256 devices in a mesh: row: 32 (over z_lo, x, core), col: 8 (over z_hi, y).
Axes of the slice: x: 4, y: 4, z: 8 (z_hi: 2, z_lo: 4; z = z_hi * 4 + z_lo), core: 2. Of those that a mesh axis runs over, the one named last changes fastest.
Arguments:
- pair: bfloat16 [512, 512, 128], P('row', 'col'), may hold values from -6 to 6
- cotangent: bfloat16 [64, 512, 512], P(None, 'row', 'col'), may hold values from -0.59765625 to 0.59765625
- w_left: bfloat16 [128, 64], replicated, may hold values from -0.5 to 0.5
- w_left_gate: bfloat16 [128, 64], replicated, may hold values from -0.5 to 0.5
- w_right: bfloat16 [128, 64], replicated, may hold values from -0.5 to 0.5
- w_right_gate: bfloat16 [128, 64], replicated, may hold values from -0.5 to 0.5
Outputs:
- pair_gradient: bfloat16 [512, 512, 128], P('row', 'col')
- grad_left: float32 [128, 64], replicated
- grad_left_gate: float32 [128, 64], replicated
- grad_right: float32 [128, 64], replicated
- grad_right_gate: float32 [128, 64], replicated
The draws below stay inside these ranges and needn't reach their ends.
All inputs are finite; a program needn't handle non-finite values.
Results may differ from the reference program's by a relative error of at most 0.0082.
Values may be sent and summed in bfloat16 or wider, within the bound.
A program may use at most 64 MiB of HBM per device.

```python
import jax
import jax.numpy as jnp
from jax import lax

N = 512
C = 128
H = 64


def block_scale(key, shape, cuts, smallest, high):
    gain, own = 1.0, jax.random.fold_in(key, 6)
    for position, blocks in cuts:
        draws = jnp.exp(jax.random.uniform(jax.random.fold_in(own, position), (blocks,), jnp.float32, smallest / len(cuts), high / len(cuts)))
        gain = gain * jnp.repeat(draws, shape[position] // blocks).reshape([-1 if axis == position else 1 for axis in range(len(shape))])
    return gain


def bell_draw(own_key, extent, scale, reach, cuts=(), dtype=jnp.bfloat16):
    result = jax.random.normal(own_key, extent, jnp.float32) * scale
    if len(cuts) > 0:
        result = block_scale(own_key, extent, cuts, -0.22, 0.18) * result
    return jnp.clip(result, min=-reach, max=reach).astype(dtype)


def setup_inputs(seed: int = 0) -> dict:
    seeds = jax.random.split(jax.random.key(seed), 7)
    return {
        "pair": bell_draw(seeds[0], (N, N, C), 1.0, 6.0, ((0, 32), (1, 8))),
        "cotangent": bell_draw(seeds[1], (H, N, N), 0.1, 0.59765625, ((1, 32), (2, 8))),
        "w_left": bell_draw(seeds[2], (C, H), C ** -0.5, 0.5),
        "w_left_gate": bell_draw(seeds[3], (C, H), C ** -0.5, 0.5),
        "w_right": bell_draw(seeds[4], (C, H), C ** -0.5, 0.5),
        "w_right_gate": bell_draw(seeds[5], (C, H), C ** -0.5, 0.5),
    }


def reference(pair, cotangent, w_left, w_left_gate, w_right, w_right_gate):
    pair_f = pair.astype(jnp.float32)
    average = lax.optimization_barrier(jnp.mean(pair_f, axis=-1, keepdims=True))
    centered_input = pair_f - average
    variance = lax.optimization_barrier(jnp.mean(centered_input * centered_input, axis=-1, keepdims=True))
    inverse_scale = 1.0 / jnp.sqrt(variance + 1e-05)
    standardized_input = centered_input * inverse_scale
    normalized_input = standardized_input.astype(jnp.bfloat16)
    stacked = jnp.concatenate([w_left, w_left_gate, w_right, w_right_gate], axis=1)
    projected = jnp.einsum('ijd,dh->hij', normalized_input.astype(jnp.float32), stacked.astype(jnp.float32))
    q_left, p_left, q_right, p_right = jnp.split(projected, 4, axis=0)
    s_left = jax.nn.sigmoid(p_left)
    s_right = jax.nn.sigmoid(p_right)
    left = (s_left * q_left).astype(jnp.bfloat16)
    right = (s_right * q_right).astype(jnp.bfloat16)

    def per_channel(items):
        g_one, l_one, r_one = items
        d_l = jnp.dot(g_one, r_one, preferred_element_type=jnp.float32)
        d_r = jnp.dot(g_one.T, l_one, preferred_element_type=jnp.float32)
        return (d_l.astype(jnp.bfloat16), d_r.astype(jnp.bfloat16))
    d_left, d_right = lax.map(per_channel, (cotangent, left, right))
    grad_l = d_left.astype(jnp.float32)
    grad_r = d_right.astype(jnp.float32)
    e_left = grad_l * s_left
    f_left = grad_l * q_left * s_left * (1.0 - s_left)
    e_right = grad_r * s_right
    f_right = grad_r * q_right * s_right * (1.0 - s_right)
    grads = jnp.concatenate([e_left, f_left, e_right, f_right], axis=0).astype(jnp.bfloat16)
    weight_grads = jnp.einsum('ijd,hij->dh', normalized_input.astype(jnp.float32), grads.astype(jnp.float32)) / N
    normalized_gradient = jnp.einsum('hij,dh->ijd', grads.astype(jnp.float32), stacked.astype(jnp.float32))
    gradient_mean = lax.optimization_barrier(jnp.mean(normalized_gradient, axis=-1, keepdims=True))
    gradient_input_mean = lax.optimization_barrier(jnp.mean(normalized_gradient * standardized_input, axis=-1, keepdims=True))
    pair_gradient = ((normalized_gradient - gradient_mean - standardized_input * gradient_input_mean) * inverse_scale).astype(jnp.bfloat16)
    parts = jnp.split(weight_grads, 4, axis=1)
    return (pair_gradient, parts[0], parts[1], parts[2], parts[3])
```

```python
import jax
import jax.numpy as jnp
from jax import lax
from jax.experimental import pallas as pl
from jax.experimental.pallas import tpu as pltpu
from jax.sharding import PartitionSpec as P

MESH = pl.DeviceIdType.MESH
BF, F32 = jnp.bfloat16, jnp.float32


def swap(v):
    return pltpu.roll(v, 64, v.ndim - 1)


def kernel(
    pair_hbm, cot_hbm, wl, wlg, wr, wrg,
    pg_out, o_l, o_lg, o_r, o_rg,
    pair_v, cot_v, wst, wcat, xhat, invs, scr, s_s, f_s, nblk,
    gs, gb, gg, lrs, lrb, dsd, db, efs, ws, rb, yb, ag,
    load_sem, send_sem, recv_sem,
):
    row, col = lax.axis_index("row"), lax.axis_index("col")
    zhi, y = lax.div(col, 4), lax.rem(col, 4)
    me = zhi * 32 + row
    core, chip = lax.rem(row, 2), lax.div(me, 2)

    def member(g):
        return (lax.rem(g, 32), lax.div(g, 32) * 4 + y)

    def other_y(d):
        return (row, zhi * 4 + lax.rem(y + d, 4))

    def remote(src, dst, phase, device):
        return pltpu.make_async_remote_copy(
            src_ref=src, dst_ref=dst, send_sem=send_sem.at[phase], recv_sem=recv_sem.at[phase],
            device_id=device, device_id_type=MESH,
        )

    load_pair = pltpu.make_async_copy(pair_hbm, pair_v, load_sem.at[0])
    load_cot = pltpu.make_async_copy(cot_hbm, cot_v, load_sem.at[1])
    load_cot.start()
    load_pair.start()

    barrier = pltpu.get_barrier_semaphore()

    def greet(d, c):
        pl.semaphore_signal(
            barrier, inc=1, device_id=member(lax.rem(me + d, 64)), device_id_type=MESH
        )
        return c

    lax.fori_loop(1, 64, greet, 0)
    for d in (1, 2, 3):
        pl.semaphore_signal(barrier, inc=1, device_id=other_y(d), device_id_type=MESH)

    wst[0:64], wst[64:128], wst[128:192], wst[192:256] = wl[...], wlg[...], wr[...], wrg[...]
    wcat[0:64, 0:128], wcat[0:64, 128:256] = wr[...], wl[...]
    wcat[64:128, 0:128], wcat[64:128, 128:256] = wrg[...], wlg[...]

    load_cot.wait()

    def pack(t, c):
        g = cot_v[pl.ds(t * 8, 8)].astype(F32)
        gs[pl.ds(t * 8, 8)] = jnp.concatenate([g[:, :8], g[:, 8:]], axis=-1).astype(BF)
        return c

    lax.fori_loop(0, 8, pack, 0)
    load_pair.wait()

    low = lax.broadcasted_iota(jnp.int32, (64, 128), 1) < 64

    def project(b, c):
        x = pair_v[pl.ds(2 * b, 2)].astype(F32).reshape(128, 128)
        cen = x - jnp.mean(x, axis=1, keepdims=True)
        var = jnp.mean(cen * cen, axis=1, keepdims=True)
        inv = jnp.broadcast_to(1.0 / jnp.sqrt(var + 1e-05), (128, 128))
        xh = cen * inv
        xhat[pl.ds(128 * b, 128)] = xh
        invs[pl.ds(128 * b, 128)] = inv
        pt = lax.dot_general(
            wst[...], xh.astype(BF), (((1,), (1,)), ((), ())), preferred_element_type=F32
        )
        q_l, p_l, q_r, p_r = pt[0:64], pt[64:128], pt[128:192], pt[192:256]
        s_l, s_r = jax.nn.sigmoid(p_l), jax.nn.sigmoid(p_r)
        l, r = s_l * q_l, s_r * q_r
        f_l, f_r = l * (1.0 - s_l), r * (1.0 - s_r)
        scr[pl.ds(2 * b, 64, stride=16), :] = jnp.where(low, l, swap(r))
        scr[pl.ds(2 * b + 1, 64, stride=16), :] = jnp.where(low, swap(l), r)
        s_lw, s_rw, f_lw, f_rw = swap(s_l), swap(s_r), swap(f_l), swap(f_r)
        s_s[2 * b], s_s[2 * b + 1] = jnp.where(low, s_r, s_lw), jnp.where(low, s_rw, s_l)
        f_s[2 * b], f_s[2 * b + 1] = jnp.where(low, f_r, f_lw), jnp.where(low, f_rw, f_l)
        return c

    lax.fori_loop(0, 8, project, 0)

    def round_lr(t, c):
        v = scr[pl.ds(t * 128, 128), :]
        lrs[pl.ds(t * 8, 8)] = v.reshape(8, 16, 128).astype(BF)
        return c

    lax.fori_loop(0, 8, round_lr, 0)

    pl.semaphore_wait(barrier, 66)

    def scatter(src, dst, phase):
        def step(d, c):
            g = lax.rem(me + d, 64)
            remote(src.at[g], dst, phase, member(g)).start()
            return c

        lax.fori_loop(1, 64, step, 0)

    scatter(gs, gb.at[y, me], 0)
    gb[y, me] = gs[me]
    scatter(lrs, lrb.at[me], 1)
    lrb[me] = lrs[me]

    def spread(b, c):
        n = xhat[pl.ds(128 * b, 128), :].astype(BF)
        z = jnp.zeros((64, 128), BF)
        nblk[pl.ds(256 * b, 256), 0:128] = jnp.concatenate([n[:64], z, n[64:], z], axis=0)
        nblk[pl.ds(256 * b, 256), 128:256] = jnp.concatenate([z, n[:64], z, n[64:]], axis=0)
        return c

    lax.fori_loop(0, 8, spread, 0)

    remote(gs.at[pl.ds(0, 63)], gb.at[0, pl.ds(0, 63)], 0, other_y(1)).wait_recv()
    for d in (1, 2, 3):
        remote(gb.at[y], gb.at[y], 2, other_y(d)).start()
    remote(gb.at[pl.ds(0, 3)], gb.at[pl.ds(0, 3)], 2, other_y(1)).wait_recv()

    low3 = lax.broadcasted_iota(jnp.int32, (8, 8, 128), 2) < 64
    for t in range(4):
        for q in range(4):
            src = pl.ds((q // 2) * 32 + 8 * t, 8)
            a = gb[2 * (q % 2), src].astype(F32)
            b = gb[2 * (q % 2) + 1, src].astype(F32)
            top, bottom = jnp.where(low3, a, swap(b)), jnp.where(low3, swap(a), b)
            full = jnp.stack([top, bottom], axis=1).reshape(128, 128)
            gg[t * 128 : t * 128 + 128, q * 128 : q * 128 + 128] = full.astype(BF)
            gg[512 + q * 128 : 640 + q * 128, t * 128 : t * 128 + 128] = full.T.astype(BF)

    remote(lrs.at[pl.ds(0, 63)], lrb.at[pl.ds(0, 63)], 1, other_y(1)).wait_recv()
    both = jnp.concatenate(
        [lrb[0:32].reshape(512, 128), lrb[32:64].reshape(512, 128)], axis=1
    )
    low2 = lax.broadcasted_iota(jnp.int32, (128, 128), 1) < 64
    for m in range(4):
        d_l = jnp.dot(gg[128 * m : 128 * m + 128], both, preferred_element_type=F32)
        d_r = jnp.dot(gg[512 + 128 * m : 640 + 128 * m], both, preferred_element_type=F32)
        for z in range(2):
            lanes = slice(128 * z, 128 * z + 128)
            d = jnp.where(low2, d_r[:, lanes], d_l[:, lanes])
            dsd[32 * z + 8 * m : 32 * z + 8 * m + 8] = d.reshape(8, 16, 128).astype(BF)

    scatter(dsd, db.at[me], 3)
    db[me] = dsd[me]
    remote(dsd.at[pl.ds(0, 63)], db.at[pl.ds(0, 63)], 3, other_y(1)).wait_recv()

    def widen(t, c):
        scr[pl.ds(t * 128, 128), :] = db[pl.ds(t * 8, 8)].astype(F32).reshape(128, 128)
        return c

    lax.fori_loop(0, 8, widen, 0)
    for i in range(16):
        d = scr[pl.ds(i, 64, stride=16), :]
        efs[0:64, 128 * i : 128 * i + 128] = (d * s_s[i]).astype(BF)
        efs[64:128, 128 * i : 128 * i + 128] = (d * f_s[i]).astype(BF)
    wg = jnp.dot(efs[...], nblk[...], preferred_element_type=F32)
    ws[0:16] = wg[:, 0:128].reshape(16, 8, 128)
    ws[16:32] = wg[:, 128:256].reshape(16, 8, 128)

    def reduce_to(d, c):
        t = lax.rem(chip + d, 32)
        remote(ws.at[t], rb.at[me], 4, member(2 * t)).start()
        return c

    lax.fori_loop(1, 32, reduce_to, 0)

    @pl.when(core == 1)
    def _():
        remote(ws.at[chip], rb.at[me], 4, member(2 * chip)).start()

    @pl.when(core == 0)
    def _():
        rb[me] = ws[chip]

    for b in range(8):
        part = lax.dot_general(
            efs[:, 256 * b : 256 * b + 256], wcat[...], (((0,), (0,)), ((), ())),
            preferred_element_type=F32,
        )
        dn = jnp.concatenate(
            [
                part[0:64, 0:128] + part[64:128, 128:256],
                part[128:192, 0:128] + part[192:256, 128:256],
            ],
            axis=0,
        )
        xh = xhat[128 * b : 128 * b + 128, :]
        m1 = jnp.mean(dn, axis=1, keepdims=True)
        m2 = jnp.mean(dn * xh, axis=1, keepdims=True)
        pg = (dn - m1 - xh * m2) * invs[128 * b : 128 * b + 128, :]
        pg_out[2 * b : 2 * b + 2] = pg.reshape(2, 64, 128).astype(BF)

    @pl.when(core == 0)
    def _():
        remote(rb.at[pl.ds(0, 63)], rb.at[pl.ds(0, 63)], 4, other_y(1)).wait_recv()
        yb[y] = jnp.sum(rb[...], axis=0)
        for d in (1, 2, 3):
            remote(yb.at[y], yb.at[y], 5, other_y(d)).start()
        remote(yb.at[pl.ds(0, 3)], yb.at[pl.ds(0, 3)], 5, other_y(1)).wait_recv()
        ag[chip] = ((yb[0] + yb[1]) + (yb[2] + yb[3])) * (1.0 / 512)

        def share(d, c):
            remote(ag.at[chip], ag.at[chip], 6, member(lax.rem(me + d, 64))).start()
            return c

        lax.fori_loop(1, 64, share, 0)
        remote(ag.at[pl.ds(0, 31)], ag.at[pl.ds(0, 31)], 6, other_y(1)).wait_recv()
        remote(rb.at[pl.ds(0, 63)], rb.at[pl.ds(0, 63)], 6, other_y(1)).wait_send()
        remote(yb.at[pl.ds(0, 3)], yb.at[pl.ds(0, 3)], 5, other_y(1)).wait_send()
        remote(ws.at[pl.ds(0, 31)], ws.at[pl.ds(0, 31)], 4, other_y(1)).wait_send()

    @pl.when(core == 1)
    def _():
        remote(ag, ag, 6, other_y(1)).wait_recv()
        remote(ws, ws, 4, other_y(1)).wait_send()

    o_r[...] = ag[0:8].reshape(64, 128)
    o_rg[...] = ag[8:16].reshape(64, 128)
    o_l[...] = ag[16:24].reshape(64, 128)
    o_lg[...] = ag[24:32].reshape(64, 128)

    remote(gs.at[pl.ds(0, 63)], gs.at[pl.ds(0, 63)], 0, other_y(1)).wait_send()
    remote(lrs.at[pl.ds(0, 63)], lrs.at[pl.ds(0, 63)], 1, other_y(1)).wait_send()
    remote(gb.at[pl.ds(0, 3)], gb.at[pl.ds(0, 3)], 2, other_y(1)).wait_send()
    remote(dsd.at[pl.ds(0, 63)], dsd.at[pl.ds(0, 63)], 3, other_y(1)).wait_send()


def shards(pair, cotangent, w_left, w_left_gate, w_right, w_right_gate):
    vm = pltpu.VMEM
    grad = jax.ShapeDtypeStruct((64, 128), F32)
    pg, g_l, g_lg, g_r, g_rg = pl.pallas_call(
        kernel,
        out_shape=[jax.ShapeDtypeStruct((16, 64, 128), BF), grad, grad, grad, grad],
        in_specs=[pl.BlockSpec(memory_space=pl.ANY)] * 2 + [pl.BlockSpec(memory_space=vm)] * 4,
        out_specs=[pl.BlockSpec(memory_space=vm)] * 5,
        scratch_shapes=[
            vm((16, 64, 128), BF),
            vm((64, 16, 64), BF),
            vm((256, 128), BF),
            vm((128, 256), BF),
            vm((1024, 128), F32),
            vm((1024, 128), F32),
            vm((1024, 128), F32),
            vm((16, 64, 128), F32),
            vm((16, 64, 128), F32),
            vm((2048, 256), BF),
            vm((64, 8, 128), BF),
            vm((4, 64, 8, 128), BF),
            vm((1024, 512), BF),
            vm((64, 16, 128), BF),
            vm((64, 16, 128), BF),
            vm((64, 16, 128), BF),
            vm((64, 16, 128), BF),
            vm((128, 2048), BF),
            vm((32, 8, 128), F32),
            vm((64, 8, 128), F32),
            vm((4, 8, 128), F32),
            vm((32, 8, 128), F32),
            pltpu.SemaphoreType.DMA((2,)),
            pltpu.SemaphoreType.DMA((7,)),
            pltpu.SemaphoreType.DMA((7,)),
        ],
        compiler_params=pltpu.CompilerParams(collective_id=0, has_side_effects=True),
    )(pair, cotangent, w_left.T, w_left_gate.T, w_right.T, w_right_gate.T)
    return pg, g_l.T, g_lg.T, g_r.T, g_rg.T


def solution(mesh):
    in_specs = (P("row", "col", None), P(None, "row", "col"), P(), P(), P(), P())
    out_specs = (P("row", "col", None), P(), P(), P(), P())
    return jax.shard_map(shards, mesh=mesh, in_specs=in_specs, out_specs=out_specs, check_vma=False)
```

```python
import jax
import jax.numpy as jnp
from jax import lax
from jax.experimental import pallas as pl
from jax.experimental.pallas import tpu as pltpu
from jax.sharding import PartitionSpec as P

MESH = pl.DeviceIdType.MESH
BF, F32 = jnp.bfloat16, jnp.float32


def swap(v):
    return pltpu.roll(v, 64, v.ndim - 1)


def kernel(
    pair_hbm, cot_hbm, wl, wlg, wr, wrg, pg_out, sums_out,
    pair_v, cot_v, wst, wcat, xhat, invs, scr, s_s, f_s, nblk,
    gs, gb, gg, lrs, lrb, dsd, db, efs, ws, rb, yb, ag,
    load_sem, send_sem, recv_sem,
):
    row, col = lax.axis_index("row"), lax.axis_index("col")
    zhi, y = lax.div(col, 4), lax.rem(col, 4)
    me = zhi * 32 + row
    z, spot = zhi * 4 + lax.div(row, 8), lax.rem(row, 8)
    place = y * 8 + spot

    def member(g):
        return (lax.rem(g, 32), lax.div(g, 32) * 4 + y)

    def other_y(d):
        return (row, zhi * 4 + lax.rem(y + d, 4))

    def other_z(d):
        t = lax.rem(z + d, 8)
        return (lax.rem(t, 4) * 8 + spot, lax.div(t, 4) * 4 + y)

    def in_plane(p):
        return (row - spot + lax.rem(p, 8), zhi * 4 + lax.div(p, 8))

    def remote(src, dst, phase, device):
        return pltpu.make_async_remote_copy(
            src_ref=src, dst_ref=dst, send_sem=send_sem.at[phase], recv_sem=recv_sem.at[phase],
            device_id=device, device_id_type=MESH,
        )

    sent = [
        gs.at[pl.ds(0, 63)], lrs.at[pl.ds(0, 63)], gb.at[pl.ds(0, 3)], dsd.at[pl.ds(0, 63)],
        ws.at[pl.ds(0, 31)], yb.at[pl.ds(0, 7)], ag.at[pl.ds(0, 31)],
    ]

    def drain(phases):
        for k in phases:
            remote(sent[k], sent[k], k, other_y(1)).wait_send()

    load_pair = pltpu.make_async_copy(pair_hbm, pair_v, load_sem.at[0])
    load_cot = pltpu.make_async_copy(cot_hbm, cot_v, load_sem.at[1])
    load_cot.start()
    load_pair.start()

    barrier = pltpu.get_barrier_semaphore()

    def greet(d, c):
        pl.semaphore_signal(
            barrier, inc=1, device_id=member(lax.rem(me + d, 64)), device_id_type=MESH
        )
        return c

    lax.fori_loop(1, 64, greet, 0)

    def greet_plane(d, c):
        p = lax.rem(y * 8 + d, 32)
        pl.semaphore_signal(barrier, inc=1, device_id=in_plane(p), device_id_type=MESH)
        return c

    lax.fori_loop(8, 32, greet_plane, 0)

    wst[0:64], wst[64:128], wst[128:192], wst[192:256] = wl[...], wlg[...], wr[...], wrg[...]
    wcat[0:64, 0:128], wcat[0:64, 128:256] = wr[...], wl[...]
    wcat[64:128, 0:128], wcat[64:128, 128:256] = wrg[...], wlg[...]

    load_cot.wait()

    def pack(t, c):
        g = cot_v[pl.ds(t * 8, 8)].astype(F32)
        gs[pl.ds(t * 8, 8)] = jnp.concatenate([g[:, :8], g[:, 8:]], axis=-1).astype(BF)
        return c

    lax.fori_loop(0, 8, pack, 0)
    load_pair.wait()

    low = lax.broadcasted_iota(jnp.int32, (64, 128), 1) < 64

    def project(b, c):
        x = pair_v[pl.ds(2 * b, 2)].astype(F32).reshape(128, 128)
        cen = x - jnp.mean(x, axis=1, keepdims=True)
        var = jnp.mean(cen * cen, axis=1, keepdims=True)
        inv = jnp.broadcast_to(1.0 / jnp.sqrt(var + 1e-05), (128, 128))
        xh = cen * inv
        xhat[pl.ds(128 * b, 128)] = xh
        invs[pl.ds(128 * b, 128)] = inv
        pt = lax.dot_general(
            wst[...], xh.astype(BF), (((1,), (1,)), ((), ())), preferred_element_type=F32
        )
        q_l, p_l, q_r, p_r = pt[0:64], pt[64:128], pt[128:192], pt[192:256]
        s_l, s_r = jax.nn.sigmoid(p_l), jax.nn.sigmoid(p_r)
        l, r = s_l * q_l, s_r * q_r
        f_l, f_r = l * (1.0 - s_l), r * (1.0 - s_r)
        scr[pl.ds(2 * b, 64, stride=16), :] = jnp.where(low, l, swap(r))
        scr[pl.ds(2 * b + 1, 64, stride=16), :] = jnp.where(low, swap(l), r)
        s_lw, s_rw, f_lw, f_rw = swap(s_l), swap(s_r), swap(f_l), swap(f_r)
        s_s[2 * b], s_s[2 * b + 1] = jnp.where(low, s_r, s_lw), jnp.where(low, s_rw, s_l)
        f_s[2 * b], f_s[2 * b + 1] = jnp.where(low, f_r, f_lw), jnp.where(low, f_rw, f_l)
        return c

    lax.fori_loop(0, 8, project, 0)

    def round_lr(t, c):
        v = scr[pl.ds(t * 128, 128), :]
        lrs[pl.ds(t * 8, 8)] = v.reshape(8, 16, 128).astype(BF)
        return c

    lax.fori_loop(0, 8, round_lr, 0)

    pl.semaphore_wait(barrier, 87)

    def scatter(src, dst, phase):
        def step(d, c):
            g = lax.rem(me + d, 64)
            remote(src.at[g], dst, phase, member(g)).start()
            return c

        lax.fori_loop(1, 64, step, 0)

    scatter(gs, gb.at[y, me], 0)
    gb[y, me] = gs[me]
    scatter(lrs, lrb.at[me], 1)
    lrb[me] = lrs[me]

    def spread(b, c):
        n = xhat[pl.ds(128 * b, 128), :].astype(BF)
        z = jnp.zeros((64, 128), BF)
        nblk[pl.ds(256 * b, 256), 0:128] = jnp.concatenate([n[:64], z, n[64:], z], axis=0)
        nblk[pl.ds(256 * b, 256), 128:256] = jnp.concatenate([z, n[:64], z, n[64:]], axis=0)
        return c

    lax.fori_loop(0, 8, spread, 0)

    remote(gs.at[pl.ds(0, 63)], gb.at[0, pl.ds(0, 63)], 0, other_y(1)).wait_recv()
    for d in (1, 2, 3):
        remote(gb.at[y], gb.at[y], 2, other_y(d)).start()
    remote(gb.at[pl.ds(0, 3)], gb.at[pl.ds(0, 3)], 2, other_y(1)).wait_recv()

    low3 = lax.broadcasted_iota(jnp.int32, (8, 8, 128), 2) < 64
    for t in range(4):
        for q in range(4):
            src = pl.ds((q // 2) * 32 + 8 * t, 8)
            a = gb[2 * (q % 2), src].astype(F32)
            b = gb[2 * (q % 2) + 1, src].astype(F32)
            top, bottom = jnp.where(low3, a, swap(b)), jnp.where(low3, swap(a), b)
            full = jnp.stack([top, bottom], axis=1).reshape(128, 128)
            gg[t * 128 : t * 128 + 128, q * 128 : q * 128 + 128] = full.astype(BF)
            gg[512 + q * 128 : 640 + q * 128, t * 128 : t * 128 + 128] = full.T.astype(BF)

    remote(lrs.at[pl.ds(0, 63)], lrb.at[pl.ds(0, 63)], 1, other_y(1)).wait_recv()
    both = jnp.concatenate(
        [lrb[0:32].reshape(512, 128), lrb[32:64].reshape(512, 128)], axis=1
    )
    low2 = lax.broadcasted_iota(jnp.int32, (128, 128), 1) < 64
    for m in range(4):
        d_l = jnp.dot(gg[128 * m : 128 * m + 128], both, preferred_element_type=F32)
        d_r = jnp.dot(gg[512 + 128 * m : 640 + 128 * m], both, preferred_element_type=F32)
        for half in range(2):
            lanes = slice(128 * half, 128 * half + 128)
            d = jnp.where(low2, d_r[:, lanes], d_l[:, lanes])
            dsd[32 * half + 8 * m : 32 * half + 8 * m + 8] = d.reshape(8, 16, 128).astype(BF)

    scatter(dsd, db.at[me], 3)
    db[me] = dsd[me]
    remote(dsd.at[pl.ds(0, 63)], db.at[pl.ds(0, 63)], 3, other_y(1)).wait_recv()

    def widen(t, c):
        scr[pl.ds(t * 128, 128), :] = db[pl.ds(t * 8, 8)].astype(F32).reshape(128, 128)
        return c

    lax.fori_loop(0, 8, widen, 0)
    for i in range(16):
        d = scr[pl.ds(i, 64, stride=16), :]
        efs[0:64, 128 * i : 128 * i + 128] = (d * s_s[i]).astype(BF)
        efs[64:128, 128 * i : 128 * i + 128] = (d * f_s[i]).astype(BF)
    wg = jnp.dot(efs[...], nblk[...], preferred_element_type=F32)
    ws[0:16] = wg[:, 0:128].reshape(16, 8, 128)
    ws[16:32] = wg[:, 128:256].reshape(16, 8, 128)

    def reduce_to(d, c):
        p = lax.rem(place + d, 32)
        remote(ws.at[p], rb.at[place], 4, in_plane(p)).start()
        return c

    lax.fori_loop(1, 32, reduce_to, 0)
    rb[place] = ws[place]

    for b in range(8):
        part = lax.dot_general(
            efs[:, 256 * b : 256 * b + 256], wcat[...], (((0,), (0,)), ((), ())),
            preferred_element_type=F32,
        )
        dn = jnp.concatenate(
            [
                part[0:64, 0:128] + part[64:128, 128:256],
                part[128:192, 0:128] + part[192:256, 128:256],
            ],
            axis=0,
        )
        xh = xhat[128 * b : 128 * b + 128, :]
        m1 = jnp.mean(dn, axis=1, keepdims=True)
        m2 = jnp.mean(dn * xh, axis=1, keepdims=True)
        pg = (dn - m1 - xh * m2) * invs[128 * b : 128 * b + 128, :]
        pg_out[2 * b : 2 * b + 2] = pg.reshape(2, 64, 128).astype(BF)

    remote(rb.at[pl.ds(0, 31)], rb.at[pl.ds(0, 31)], 4, other_y(1)).wait_recv()
    yb[z] = jnp.sum(rb[...], axis=0)
    for d in range(1, 8):
        remote(yb.at[z], yb.at[z], 5, other_z(d)).start()
    remote(yb.at[pl.ds(0, 7)], yb.at[pl.ds(0, 7)], 5, other_y(1)).wait_recv()
    ag[place] = jnp.sum(yb[...], axis=0) * (1.0 / 512)

    def share(d, c):
        remote(ag.at[place], ag.at[place], 6, in_plane(lax.rem(place + d, 32))).start()
        return c

    lax.fori_loop(1, 32, share, 0)
    remote(ag.at[pl.ds(0, 31)], ag.at[pl.ds(0, 31)], 6, other_y(1)).wait_recv()
    sums_out[...] = ag[...]
    drain(range(7))


def deliver(pg, sums, out, *rest):
    sem = rest[-1]
    copies = [pltpu.make_async_copy(pg, out, sem.at[0])]
    for k in range(4):
        copies.append(pltpu.make_async_copy(sums.at[pl.ds(8 * k, 8)], rest[k], sem.at[k + 1]))
    for copy in copies:
        copy.start()
    for copy in copies:
        copy.wait()


def shards(pair, cotangent, w_left, w_left_gate, w_right, w_right_gate):
    vm = pltpu.VMEM
    pg, sums = pl.pallas_call(
        kernel,
        out_shape=[vm((16, 64, 128), BF), vm((32, 8, 128), F32)],
        in_specs=[pl.BlockSpec(memory_space=pl.ANY)] * 2 + [pl.BlockSpec(memory_space=vm)] * 4,
        out_specs=[pl.BlockSpec(memory_space=vm)] * 2,
        scratch_shapes=[
            vm((16, 64, 128), BF),
            vm((64, 16, 64), BF),
            vm((256, 128), BF),
            vm((128, 256), BF),
            vm((1024, 128), F32),
            vm((1024, 128), F32),
            vm((1024, 128), F32),
            vm((16, 64, 128), F32),
            vm((16, 64, 128), F32),
            vm((2048, 256), BF),
            vm((64, 8, 128), BF),
            vm((4, 64, 8, 128), BF),
            vm((1024, 512), BF),
            vm((64, 16, 128), BF),
            vm((64, 16, 128), BF),
            vm((64, 16, 128), BF),
            vm((64, 16, 128), BF),
            vm((128, 2048), BF),
            vm((32, 8, 128), F32),
            vm((32, 8, 128), F32),
            vm((8, 8, 128), F32),
            vm((32, 8, 128), F32),
            pltpu.SemaphoreType.DMA((2,)),
            pltpu.SemaphoreType.DMA((7,)),
            pltpu.SemaphoreType.DMA((7,)),
        ],
        compiler_params=pltpu.CompilerParams(collective_id=0, has_side_effects=True),
    )(pair, cotangent, w_left.T, w_left_gate.T, w_right.T, w_right_gate.T)
    keep = pltpu.with_memory_space_constraint
    grad = jax.ShapeDtypeStruct((8, 8, 128), F32)
    out, g_r, g_rg, g_l, g_lg = pl.pallas_call(
        deliver,
        out_shape=[jax.ShapeDtypeStruct((16, 64, 128), BF), grad, grad, grad, grad],
        in_specs=[pl.BlockSpec(memory_space=vm)] * 2,
        out_specs=[pl.BlockSpec(memory_space=pl.ANY)] * 5,
        scratch_shapes=[pltpu.SemaphoreType.DMA((5,))],
    )(keep(pg, vm), keep(sums, vm))
    return (out, *(g.reshape(64, 128).T for g in (g_l, g_lg, g_r, g_rg)))


def solution(mesh):
    in_specs = (P("row", "col", None), P(None, "row", "col"), P(), P(), P(), P())
    out_specs = (P("row", "col", None), P(), P(), P(), P())
    return jax.shard_map(shards, mesh=mesh, in_specs=in_specs, out_specs=out_specs, check_vma=False)
```

```python
import jax
import jax.numpy as jnp
from jax import lax
from jax.experimental import pallas as pl
from jax.experimental.pallas import tpu as pltpu
from jax.sharding import PartitionSpec as P

MESH = pl.DeviceIdType.MESH
BF, F32 = jnp.bfloat16, jnp.float32

G_OWN, R_OWN, G_ALL, L_OWN, D_LEFT, D_RIGHT, W_PLANE, W_Z, W_ALL = range(9)


def swap(v):
    return pltpu.roll(v, 64, v.ndim - 1)


def kernel(
    pair_hbm, cot_hbm, wl, wlg, wr, wrg, pg_out, sums_out,
    pair_v, cot_v, wst, xhat, invs, nrm, scr, s_s, f_s,
    gs, gb, gg, rs, rb, ls, lb, mat, dls, dlb, drs, drb, efs, ws, wb, zb, ag,
    load_sem, send_sem, recv_sem, g_sem,
):
    row, col = lax.axis_index("row"), lax.axis_index("col")
    zhi, y = lax.div(col, 4), lax.rem(col, 4)
    z, spot = zhi * 4 + lax.div(row, 8), lax.rem(row, 8)
    core = lax.rem(spot, 2)
    me = z * 8 + spot
    place = y * 8 + spot
    pair_of = lax.div(place, 2)

    def member(g):
        return (lax.rem(g, 32), lax.div(g, 32) * 4 + y)

    def other_y(d):
        return (row, zhi * 4 + lax.rem(y + d, 4))

    def in_plane(p):
        return (row - spot + lax.rem(p, 8), zhi * 4 + lax.div(p, 8))

    def far_first(i):
        k = lax.div(i, 8)
        dz = 4 + (1 - 2 * lax.rem(k, 2)) * lax.div(k + 1, 2)
        e = lax.rem(i, 8) + lax.div(i, 56)
        return lax.rem(z + dz, 8) * 8 + lax.rem(spot + e, 8)

    def remote(src, dst, phase, device, arrival=None):
        return pltpu.make_async_remote_copy(
            src_ref=src, dst_ref=dst, send_sem=send_sem.at[phase],
            recv_sem=recv_sem.at[phase] if arrival is None else arrival,
            device_id=device, device_id_type=MESH,
        )

    def arrived(ref, phase, arrival=None):
        remote(ref, ref, phase, other_y(1), arrival).wait_recv()

    def scatter(src, dst, phase, arrival=None):
        def step(i, c):
            g = far_first(i)
            remote(src.at[g], dst, phase, member(g), arrival).start()
            return c

        lax.fori_loop(0, 63, step, 0)

    most = pl.ds(0, 63)
    sent = [
        gs.at[most], rs.at[most], gb.at[pl.ds(0, 3)], ls.at[most], dls.at[most], drs.at[most],
        wb.at[pl.ds(0, 31)], zb.at[pl.ds(0, 7)], wb.at[pl.ds(0, 31)],
    ]

    def drain(phases):
        for k in phases:
            remote(sent[k], sent[k], k, other_y(1)).wait_send()

    barrier = pltpu.get_barrier_semaphore()

    def greet(i, c):
        pl.semaphore_signal(
            barrier, inc=1, device_id=member(far_first(i)), device_id_type=MESH
        )
        return c

    lax.fori_loop(0, 63, greet, 0)

    def greet_plane(d, c):
        p = lax.rem(y * 8 + d, 32)
        pl.semaphore_signal(barrier, inc=1, device_id=in_plane(p), device_id_type=MESH)
        return c

    lax.fori_loop(8, 32, greet_plane, 0)

    loads = [
        pltpu.make_async_copy(cot_hbm, cot_v, load_sem.at[0]),
        pltpu.make_async_copy(pair_hbm, pair_v, load_sem.at[1]),
    ]
    for k, w in enumerate((wl, wlg, wr, wrg)):
        loads.append(pltpu.make_async_copy(w, wst.at[pl.ds(64 * k, 64)], load_sem.at[2 + k]))
    for load in loads:
        load.start()

    loads[0].wait()

    def pack(t, c):
        g = cot_v[pl.ds(t * 8, 8)].astype(F32)
        gs[pl.ds(t * 8, 8)] = jnp.concatenate([g[:, :8], g[:, 8:]], axis=-1).astype(BF)
        return c

    lax.fori_loop(0, 8, pack, 0, unroll=2)
    gb[y, me] = gs[me]
    for load in loads[1:]:
        load.wait()

    def gated(side, b, n):
        pt = lax.dot_general(
            wst[128 * side : 128 * side + 128], n, (((1,), (1,)), ((), ())),
            preferred_element_type=F32,
        )
        q, s = pt[:64], jax.nn.sigmoid(pt[64:])
        v = s * q
        s_s[side, b] = s
        f_s[side, b] = v * (1.0 - s)
        scr[side, pl.ds(b, 64, stride=8), :] = v

    def normalize(b, c):
        x = jnp.concatenate([pair_v[b], pair_v[b + 8]], axis=0).astype(F32)
        cen = x - jnp.mean(x, axis=1, keepdims=True)
        var = jnp.mean(cen * cen, axis=1, keepdims=True)
        inv = jnp.broadcast_to(1.0 / jnp.sqrt(var + 1e-05), (128, 128))
        xh = cen * inv
        n = xh.astype(BF)
        xhat[pl.ds(128 * b, 128)] = xh
        invs[pl.ds(128 * b, 128)] = inv
        nrm[pl.ds(128 * b, 128)] = n
        gated(1, b, n)
        return c

    lax.fori_loop(0, 8, normalize, 0, unroll=4)
    rs[...] = scr[1].reshape(64, 8, 128).astype(BF)
    rb[me] = rs[me]
    pl.semaphore_wait(barrier, 87)
    scatter(gs, gb.at[y, me], G_OWN, g_sem.at[z])
    scatter(rs, rb.at[me], R_OWN)

    def left_too(b, c):
        gated(0, b, nrm[pl.ds(128 * b, 128)])
        return c

    lax.fori_loop(0, 8, left_too, 0, unroll=4)
    ls[...] = scr[0].reshape(64, 8, 128).astype(BF)
    lb[me] = ls[me]
    scatter(ls, lb.at[me], L_OWN)

    def spread(zz):
        block = gb.at[y, pl.ds(zz * 8, 8)]
        for d in (1, 2, 3):
            remote(block, block, G_ALL, other_y(d)).start()

    arrived(gb.at[0, pl.ds(0, 7)], G_OWN, g_sem.at[z])
    spread(z)

    def spread_next(k, c):
        zz = lax.rem(z + 8 + (2 * lax.rem(k, 2) - 1) * lax.div(k + 1, 2), 8)
        arrived(gb.at[0, pl.ds(0, 8)], G_OWN, g_sem.at[zz])
        spread(zz)
        return c

    lax.fori_loop(1, 8, spread_next, 0)
    arrived(gb.at[pl.ds(0, 3)], G_ALL)

    low3 = lax.broadcasted_iota(jnp.int32, (8, 8, 128), 2) < 64

    def interleave(a, b):
        a, b = a.astype(F32), b.astype(F32)
        top, bottom = jnp.where(low3, a, swap(b)), jnp.where(low3, swap(a), b)
        return jnp.stack([top, bottom], axis=1).reshape(128, 128).astype(BF)

    for t in range(4):
        for q in range(4):
            src = pl.ds((q // 2) * 32 + 8 * t, 8)
            gg[t * 128 : t * 128 + 128, q * 128 : q * 128 + 128] = interleave(
                gb[2 * (q % 2), src], gb[2 * (q % 2) + 1, src]
            )

    def contract(first, got, dst):
        for t in range(4):
            mat[128 * t : 128 * t + 128] = interleave(
                got[8 * t : 8 * t + 8], got[32 + 8 * t : 40 + 8 * t]
            )
        for m in range(4):
            d = jnp.dot(
                gg[first + 128 * m : first + 128 * m + 128], mat[...],
                preferred_element_type=F32,
            ).reshape(8, 2, 8, 128)
            a, b = d[:, 0], d[:, 1]
            dst[8 * m : 8 * m + 8] = jnp.where(low3, a, swap(b)).astype(BF)
            dst[32 + 8 * m : 40 + 8 * m] = jnp.where(low3, swap(a), b).astype(BF)

    arrived(rb.at[most], R_OWN)
    contract(0, rb, dls)
    scatter(dls, dlb.at[me], D_LEFT)
    dlb[me] = dls[me]

    for t in range(4):
        for q in range(4):
            block = gg[t * 128 : t * 128 + 128, q * 128 : q * 128 + 128]
            gg[512 + q * 128 : 640 + q * 128, t * 128 : t * 128 + 128] = block.T
    arrived(lb.at[most], L_OWN)
    contract(512, lb, drs)
    scatter(drs, drb.at[me], D_RIGHT)
    drb[me] = drs[me]

    def weigh(side, got):
        scr[side] = got[...].astype(F32).reshape(512, 128)
        e, f = 128 * side, 128 * side + 64
        for b in range(8):
            d = scr[side, pl.ds(b, 64, stride=8), :]
            efs[e : e + 64, 128 * b : 128 * b + 128] = (d * s_s[side, b]).astype(BF)
            efs[f : f + 64, 128 * b : 128 * b + 128] = (d * f_s[side, b]).astype(BF)
        wg = jnp.dot(efs[e : e + 128], nrm[...], preferred_element_type=F32)
        ws[:, side] = wg.reshape(16, 8, 128)

        def reduce_to(d, c):
            p = lax.rem(pair_of + d, 16)
            remote(ws.at[p, side], wb.at[place], W_PLANE, in_plane(2 * p + side)).start()
            return c

        lax.fori_loop(1, 16, reduce_to, 0)

        @pl.when(core != side)
        def _():
            own = in_plane(2 * pair_of + side)
            remote(ws.at[pair_of, side], wb.at[place], W_PLANE, own).start()

        @pl.when(core == side)
        def _():
            wb[place] = ws[pair_of, side]

    arrived(dlb.at[most], D_LEFT)
    weigh(0, dlb)
    arrived(drb.at[most], D_RIGHT)
    weigh(1, drb)
    for b in range(8):
        dn = lax.dot_general(
            efs[:, 128 * b : 128 * b + 128], wst[...], (((0,), (0,)), ((), ())),
            preferred_element_type=F32,
        )
        xh = xhat[128 * b : 128 * b + 128, :]
        m1 = jnp.mean(dn, axis=1, keepdims=True)
        m2 = jnp.mean(dn * xh, axis=1, keepdims=True)
        pg = ((dn - m1 - xh * m2) * invs[128 * b : 128 * b + 128, :]).astype(BF)
        pg_out[b], pg_out[b + 8] = pg[:64], pg[64:]

    arrived(wb.at[pl.ds(0, 31)], W_PLANE)
    zb[z] = jnp.sum(wb[...], axis=0)
    for d in range(1, 8):
        remote(zb.at[z], zb.at[z], W_Z, member(lax.rem(me + 8 * d, 64))).start()
    arrived(zb.at[pl.ds(0, 7)], W_Z)
    ag[pair_of, core] = jnp.sum(zb[...], axis=0) * (1.0 / 512)

    def share(d, c):
        mine = ag.at[pair_of, core]
        remote(mine, mine, W_ALL, in_plane(lax.rem(place + d, 32))).start()
        return c

    lax.fori_loop(1, 32, share, 0)
    arrived(wb.at[pl.ds(0, 31)], W_ALL)
    sums_out[0:16] = ag[:, 0]
    sums_out[16:32] = ag[:, 1]
    drain(range(9))


def deliver(pg, sums, out, *rest):
    sem = rest[-1]
    copies = [pltpu.make_async_copy(pg, out, sem.at[0])]
    for k in range(4):
        copies.append(pltpu.make_async_copy(sums.at[pl.ds(8 * k, 8)], rest[k], sem.at[k + 1]))
    for copy in copies:
        copy.start()
    for copy in copies:
        copy.wait()


def shards(pair, cotangent, w_left, w_left_gate, w_right, w_right_gate):
    vm, dma = pltpu.VMEM, pltpu.SemaphoreType.DMA
    chunk = vm((64, 8, 128), BF)
    pg, sums = pl.pallas_call(
        kernel,
        out_shape=[vm((16, 64, 128), BF), vm((32, 8, 128), F32)],
        in_specs=[pl.BlockSpec(memory_space=pl.ANY)] * 6,
        out_specs=[pl.BlockSpec(memory_space=vm)] * 2,
        scratch_shapes=[
            vm((16, 64, 128), BF),
            vm((64, 16, 64), BF),
            vm((256, 128), BF),
            vm((1024, 128), F32),
            vm((1024, 128), F32),
            vm((1024, 128), BF),
            vm((2, 512, 128), F32),
            vm((2, 8, 64, 128), F32),
            vm((2, 8, 64, 128), F32),
            chunk,
            vm((4, 64, 8, 128), BF),
            vm((1024, 512), BF),
            chunk, chunk, chunk, chunk,
            vm((512, 128), BF),
            chunk, chunk, chunk, chunk,
            vm((256, 1024), BF),
            vm((16, 2, 8, 128), F32),
            vm((32, 8, 128), F32),
            vm((8, 8, 128), F32),
            vm((16, 2, 8, 128), F32),
            dma((6,)), dma((9,)), dma((9,)), dma((8,)),
        ],
        compiler_params=pltpu.CompilerParams(collective_id=0, has_side_effects=True),
    )(pair, cotangent, w_left.T, w_left_gate.T, w_right.T, w_right_gate.T)
    keep = pltpu.with_memory_space_constraint
    grad = jax.ShapeDtypeStruct((8, 8, 128), F32)
    out, *grads = pl.pallas_call(
        deliver,
        out_shape=[jax.ShapeDtypeStruct((16, 64, 128), BF), grad, grad, grad, grad],
        in_specs=[pl.BlockSpec(memory_space=vm)] * 2,
        out_specs=[pl.BlockSpec(memory_space=pl.ANY)] * 5,
        scratch_shapes=[dma((5,))],
    )(keep(pg, vm), keep(sums, vm))
    return (out, *(g.reshape(64, 128).T for g in grads))


def solution(mesh):
    in_specs = (P("row", "col", None), P(None, "row", "col"), P(), P(), P(), P())
    out_specs = (P("row", "col", None), P(), P(), P(), P())
    return jax.shard_map(shards, mesh=mesh, in_specs=in_specs, out_specs=out_specs, check_vma=False)
```

```python
import jax
import jax.numpy as jnp
from jax import lax
from jax.experimental import pallas as pl
from jax.experimental.pallas import tpu as pltpu
from jax.sharding import PartitionSpec as P

MESH = pl.DeviceIdType.MESH
BF, F32 = jnp.bfloat16, jnp.float32

G_OWN, R_OWN, G_ALL, L_OWN, D_LEFT, D_RIGHT, W_PLANE, W_Z, W_ALL = range(9)


def swap(v):
    return pltpu.roll(v, 64, v.ndim - 1)


def kernel(
    pair_hbm, cot_hbm, wl, wlg, wr, wrg, pg_out, sums_out,
    pair_v, cot_v, wst, xhat, invs, nrm, scr, s_s, f_s,
    gs, gb, gg, rs, rb, ls, lb, mat, dls, dlb, drs, drb, efs, ws, wb, zb, ag,
    load_sem, send_sem, recv_sem, g_sem, gy_sem,
):
    row, col = lax.axis_index("row"), lax.axis_index("col")
    zhi, y = lax.div(col, 4), lax.rem(col, 4)
    z, spot = zhi * 4 + lax.div(row, 8), lax.rem(row, 8)
    core = lax.rem(spot, 2)
    me = z * 8 + spot
    place = y * 8 + spot
    pair_of = lax.div(place, 2)

    def member(g):
        return (lax.rem(g, 32), lax.div(g, 32) * 4 + y)

    def other_y(d):
        return (row, zhi * 4 + lax.rem(y + d, 4))

    def in_plane(p):
        return (row - spot + lax.rem(p, 8), zhi * 4 + lax.div(p, 8))

    spots = [lax.rem(spot + e, 8) for e in range(8)]

    def near(k):
        return lax.rem(z + 8 + (2 * lax.rem(k, 2) - 1) * lax.div(k + 1, 2), 8)

    def far(k):
        return lax.rem(z + 4 + (1 - 2 * lax.rem(k, 2)) * lax.div(k + 1, 2), 8)

    def each_member(act, near_first=False):
        def of_z(zz, turn):
            r, c = lax.rem(zz, 4) * 8, lax.div(zz, 4) * 4 + y
            for e in turn:
                act(zz * 8 + spots[e], (r + spots[e], c))

        def step(k, carry):
            of_z(near(k + 1) if near_first else far(k), range(8))
            return carry

        if near_first:
            of_z(z, range(1, 8))
        lax.fori_loop(0, 7, step, 0)
        if not near_first:
            of_z(z, range(1, 8))

    def remote(src, dst, phase, device, arrival=None):
        return pltpu.make_async_remote_copy(
            src_ref=src, dst_ref=dst, send_sem=send_sem.at[phase],
            recv_sem=recv_sem.at[phase] if arrival is None else arrival,
            device_id=device, device_id_type=MESH,
        )

    def arrived(ref, phase, arrival=None):
        remote(ref, ref, phase, other_y(1), arrival).wait_recv()

    def scatter(src, dst, phase, arrival=None, near_first=False):
        def send(g, device):
            remote(src.at[g], dst, phase, device, arrival).start()

        each_member(send, near_first)

    most = pl.ds(0, 63)
    sent = [
        gs.at[most], rs.at[most], gb.at[pl.ds(0, 3)], ls.at[most], dls.at[most], drs.at[most],
        wb.at[pl.ds(0, 31)], zb.at[pl.ds(0, 7)], wb.at[pl.ds(0, 31)],
    ]

    def drain(phases):
        for k in phases:
            remote(sent[k], sent[k], k, other_y(1)).wait_send()

    barrier = pltpu.get_barrier_semaphore()

    def greet(device):
        pl.semaphore_signal(barrier, inc=1, device_id=device, device_id_type=MESH)

    each_member(lambda g, device: greet(device))

    for d in (1, 2, 3):
        for p in spots:
            greet((row - spot + p, zhi * 4 + lax.rem(y + d, 4)))

    loads = [
        pltpu.make_async_copy(cot_hbm, cot_v, load_sem.at[0]),
        pltpu.make_async_copy(pair_hbm, pair_v, load_sem.at[1]),
    ]
    for k, w in enumerate((wl, wlg, wr, wrg)):
        loads.append(pltpu.make_async_copy(w, wst.at[pl.ds(64 * k, 64)], load_sem.at[2 + k]))
    for load in loads:
        load.start()

    loads[0].wait()

    def pack(t, c):
        g = cot_v[pl.ds(t * 8, 8)].astype(F32)
        gs[pl.ds(t * 8, 8)] = jnp.concatenate([g[:, :8], g[:, 8:]], axis=-1).astype(BF)
        return c

    lax.fori_loop(0, 8, pack, 0, unroll=2)
    gb[y, me] = gs[me]
    for load in loads[1:]:
        load.wait()

    def gated(side, b, n):
        pt = lax.dot_general(
            wst[128 * side : 128 * side + 128], n, (((1,), (1,)), ((), ())),
            preferred_element_type=F32,
        )
        q, s = pt[:64], jax.nn.sigmoid(pt[64:])
        v = s * q
        s_s[side, b] = s
        f_s[side, b] = v * (1.0 - s)
        scr[side, pl.ds(b, 64, stride=8), :] = v

    def normalize(b, c):
        x = jnp.concatenate([pair_v[b], pair_v[b + 8]], axis=0).astype(F32)
        cen = x - jnp.mean(x, axis=1, keepdims=True)
        var = jnp.mean(cen * cen, axis=1, keepdims=True)
        inv = jnp.broadcast_to(1.0 / jnp.sqrt(var + 1e-05), (128, 128))
        xh = cen * inv
        n = xh.astype(BF)
        xhat[pl.ds(128 * b, 128)] = xh
        invs[pl.ds(128 * b, 128)] = inv
        nrm[pl.ds(128 * b, 128)] = n
        gated(1, b, n)
        return c

    lax.fori_loop(0, 8, normalize, 0, unroll=4)
    rs[...] = scr[1].reshape(64, 8, 128).astype(BF)
    rb[me] = rs[me]
    pl.semaphore_wait(barrier, 87)
    scatter(gs, gb.at[y, me], G_OWN, g_sem.at[z], near_first=True)
    def left_too(b, c):
        gated(0, b, nrm[pl.ds(128 * b, 128)])
        return c

    lax.fori_loop(0, 8, left_too, 0, unroll=4)
    ls[...] = scr[0].reshape(64, 8, 128).astype(BF)
    lb[me] = ls[me]
    drain([G_OWN])
    scatter(rs, rb.at[me], R_OWN)
    scatter(ls, lb.at[me], L_OWN)

    def spread(zz):
        block = gb.at[y, pl.ds(zz * 8, 8)]
        for d in (1, 2, 3):
            remote(block, block, G_ALL, other_y(d), gy_sem.at[zz]).start()

    arrived(gb.at[0, pl.ds(0, 7)], G_OWN, g_sem.at[z])
    spread(z)

    def spread_next(k, c):
        zz = near(k)
        arrived(gb.at[0, pl.ds(0, 8)], G_OWN, g_sem.at[zz])
        spread(zz)
        return c

    lax.fori_loop(1, 8, spread_next, 0)
    low3 = lax.broadcasted_iota(jnp.int32, (8, 8, 128), 2) < 64

    def interleave(a, b):
        a, b = a.astype(F32), b.astype(F32)
        top, bottom = jnp.where(low3, a, swap(b)), jnp.where(low3, swap(a), b)
        return jnp.stack([top, bottom], axis=1).reshape(128, 128).astype(BF)

    def join(side, got):
        for t in range(4):
            mat[side, 128 * t : 128 * t + 128] = interleave(
                got[8 * t : 8 * t + 8], got[32 + 8 * t : 40 + 8 * t]
            )

    def contract(side, first, dst):
        for m in range(4):
            d = jnp.dot(
                gg[first + 128 * m : first + 128 * m + 128], mat[side],
                preferred_element_type=F32,
            ).reshape(8, 2, 8, 128)
            a, b = d[:, 0], d[:, 1]
            dst[8 * m : 8 * m + 8] = jnp.where(low3, a, swap(b)).astype(BF)
            dst[32 + 8 * m : 40 + 8 * m] = jnp.where(low3, swap(a), b).astype(BF)

    def collect(k, c):
        zz = near(k)
        arrived(gb.at[0, pl.ds(0, 24)], G_ALL, gy_sem.at[zz])
        rows = pl.ds(pl.multiple_of(lax.rem(zz, 4) * 128, 128), 128)
        for q in range(2):
            lanes = pl.ds(pl.multiple_of(lax.div(zz, 4) * 256 + q * 128, 128), 128)
            src = pl.ds(zz * 8, 8)
            gg[rows, lanes] = interleave(gb[2 * q, src], gb[2 * q + 1, src])
        return c

    lax.fori_loop(0, 4, collect, 0)
    arrived(rb.at[most], R_OWN)
    join(1, rb)
    lax.fori_loop(4, 8, collect, 0)
    contract(1, 0, dls)
    scatter(dls, dlb.at[me], D_LEFT)
    dlb[me] = dls[me]

    for t in range(4):
        for q in range(4):
            block = gg[t * 128 : t * 128 + 128, q * 128 : q * 128 + 128]
            gg[512 + q * 128 : 640 + q * 128, t * 128 : t * 128 + 128] = block.T
    arrived(lb.at[most], L_OWN)
    join(0, lb)
    contract(0, 512, drs)
    scatter(drs, drb.at[me], D_RIGHT)
    drb[me] = drs[me]

    def weigh(side, got):
        scr[side] = got[...].astype(F32).reshape(512, 128)
        e, f = 128 * side, 128 * side + 64
        for b in range(8):
            d = scr[side, pl.ds(b, 64, stride=8), :]
            efs[e : e + 64, 128 * b : 128 * b + 128] = (d * s_s[side, b]).astype(BF)
            efs[f : f + 64, 128 * b : 128 * b + 128] = (d * f_s[side, b]).astype(BF)
        wg = jnp.dot(efs[e : e + 128], nrm[...], preferred_element_type=F32)
        ws[:, side] = wg.reshape(16, 8, 128)

        def reduce_to(d, c):
            p = lax.rem(pair_of + d, 16)
            remote(ws.at[p, side], wb.at[place], W_PLANE, in_plane(2 * p + side)).start()
            return c

        lax.fori_loop(1, 16, reduce_to, 0)

        @pl.when(core != side)
        def _():
            own = in_plane(2 * pair_of + side)
            remote(ws.at[pair_of, side], wb.at[place], W_PLANE, own).start()

        @pl.when(core == side)
        def _():
            wb[place] = ws[pair_of, side]

    arrived(dlb.at[most], D_LEFT)
    weigh(0, dlb)
    arrived(drb.at[most], D_RIGHT)
    weigh(1, drb)
    for b in range(8):
        dn = lax.dot_general(
            efs[:, 128 * b : 128 * b + 128], wst[...], (((0,), (0,)), ((), ())),
            preferred_element_type=F32,
        )
        xh = xhat[128 * b : 128 * b + 128, :]
        m1 = jnp.mean(dn, axis=1, keepdims=True)
        m2 = jnp.mean(dn * xh, axis=1, keepdims=True)
        pg = ((dn - m1 - xh * m2) * invs[128 * b : 128 * b + 128, :]).astype(BF)
        pg_out[b], pg_out[b + 8] = pg[:64], pg[64:]

    arrived(wb.at[pl.ds(0, 31)], W_PLANE)
    zb[z] = jnp.sum(wb[...], axis=0)
    for d in range(1, 8):
        remote(zb.at[z], zb.at[z], W_Z, member(lax.rem(me + 8 * d, 64))).start()
    arrived(zb.at[pl.ds(0, 7)], W_Z)
    ag[pair_of, core] = jnp.sum(zb[...], axis=0) * (1.0 / 512)

    def share(d, c):
        mine = ag.at[pair_of, core]
        remote(mine, mine, W_ALL, in_plane(lax.rem(place + d, 32))).start()
        return c

    lax.fori_loop(1, 32, share, 0)
    arrived(wb.at[pl.ds(0, 31)], W_ALL)
    sums_out[0:16] = ag[:, 0]
    sums_out[16:32] = ag[:, 1]
    drain(range(R_OWN, 9))


def deliver(pg, sums, out, *rest):
    sem = rest[-1]
    copies = [pltpu.make_async_copy(pg, out, sem.at[0])]
    for k in range(4):
        copies.append(pltpu.make_async_copy(sums.at[pl.ds(8 * k, 8)], rest[k], sem.at[k + 1]))
    for copy in copies:
        copy.start()
    for copy in copies:
        copy.wait()


def shards(pair, cotangent, w_left, w_left_gate, w_right, w_right_gate):
    vm, dma = pltpu.VMEM, pltpu.SemaphoreType.DMA
    chunk = vm((64, 8, 128), BF)
    pg, sums = pl.pallas_call(
        kernel,
        out_shape=[vm((16, 64, 128), BF), vm((32, 8, 128), F32)],
        in_specs=[pl.BlockSpec(memory_space=pl.ANY)] * 6,
        out_specs=[pl.BlockSpec(memory_space=vm)] * 2,
        scratch_shapes=[
            vm((16, 64, 128), BF),
            vm((64, 16, 64), BF),
            vm((256, 128), BF),
            vm((1024, 128), F32),
            vm((1024, 128), F32),
            vm((1024, 128), BF),
            vm((2, 512, 128), F32),
            vm((2, 8, 64, 128), F32),
            vm((2, 8, 64, 128), F32),
            chunk,
            vm((4, 64, 8, 128), BF),
            vm((1024, 512), BF),
            chunk, chunk, chunk, chunk,
            vm((2, 512, 128), BF),
            chunk, chunk, chunk, chunk,
            vm((256, 1024), BF),
            vm((16, 2, 8, 128), F32),
            vm((32, 8, 128), F32),
            vm((8, 8, 128), F32),
            vm((16, 2, 8, 128), F32),
            dma((6,)), dma((9,)), dma((9,)), dma((8,)), dma((8,)),
        ],
        compiler_params=pltpu.CompilerParams(collective_id=0, has_side_effects=True),
    )(pair, cotangent, w_left.T, w_left_gate.T, w_right.T, w_right_gate.T)
    keep = pltpu.with_memory_space_constraint
    grad = jax.ShapeDtypeStruct((8, 8, 128), F32)
    out, *grads = pl.pallas_call(
        deliver,
        out_shape=[jax.ShapeDtypeStruct((16, 64, 128), BF), grad, grad, grad, grad],
        in_specs=[pl.BlockSpec(memory_space=vm)] * 2,
        out_specs=[pl.BlockSpec(memory_space=pl.ANY)] * 5,
        scratch_shapes=[dma((5,))],
    )(keep(pg, vm), keep(sums, vm))
    return (out, *(g.reshape(64, 128).T for g in grads))


def solution(mesh):
    in_specs = (P("row", "col", None), P(None, "row", "col"), P(), P(), P(), P())
    out_specs = (P("row", "col", None), P(), P(), P(), P())
    return jax.shard_map(shards, mesh=mesh, in_specs=in_specs, out_specs=out_specs, check_vma=False)
```

```python
import jax
import jax.numpy as jnp
from jax import lax
from jax.experimental import pallas as pl
from jax.experimental.pallas import tpu as pltpu
from jax.sharding import PartitionSpec as P

MESH = pl.DeviceIdType.MESH
BF, F32 = jnp.bfloat16, jnp.float32

G_OWN, R_OWN, G_ALL, L_OWN, D_LEFT, D_RIGHT, W_PLANE, W_Z, W_ALL = range(9)


def swap(v):
    return pltpu.roll(v, 64, v.ndim - 1)


def kernel(
    pair_hbm, cot_hbm, wl, wlg, wr, wrg, pg_out, sums_out,
    pair_v, cot_v, wst, xhat, invs, nrm, scr, s_s, f_s,
    gs, gb, gg, rs, rb, ls, lb, mat, dls, dlb, drs, drb, efs, ws, wb, zb, ag,
    load_sem, send_sem, recv_sem, g_sem, gy_sem,
):
    row, col = lax.axis_index("row"), lax.axis_index("col")
    zhi, y = lax.div(col, 4), lax.rem(col, 4)
    z, spot = zhi * 4 + lax.div(row, 8), lax.rem(row, 8)
    core = lax.rem(spot, 2)
    me = z * 8 + spot
    place = y * 8 + spot
    pair_of = lax.div(place, 2)

    def member(g):
        return (lax.rem(g, 32), lax.div(g, 32) * 4 + y)

    def other_y(d):
        return (row, zhi * 4 + lax.rem(y + d, 4))

    def in_plane(p):
        return (row - spot + lax.rem(p, 8), zhi * 4 + lax.div(p, 8))

    spots = [lax.rem(spot + e, 8) for e in range(8)]

    def near(k):
        return lax.rem(z + 8 + (2 * lax.rem(k, 2) - 1) * lax.div(k + 1, 2), 8)

    def paired(k):
        return lax.rem(near(lax.div(k, 2)) + 4 * lax.rem(k, 2), 8)

    def far(k):
        return lax.rem(z + 4 + (1 - 2 * lax.rem(k, 2)) * lax.div(k + 1, 2), 8)

    def of_z(act, zz, turn):
        r, c = lax.rem(zz, 4) * 8, lax.div(zz, 4) * 4 + y
        for e in turn:
            act(zz * 8 + spots[e], (r + spots[e], c))

    def each_member(act, pairs=False):
        def step(k, carry):
            of_z(act, paired(k + 1) if pairs else far(k), range(8))
            return carry

        if pairs:
            of_z(act, z, range(1, 8))
        lax.fori_loop(0, 7, step, 0)
        if not pairs:
            of_z(act, z, range(1, 8))

    def remote(src, dst, phase, device, arrival=None):
        return pltpu.make_async_remote_copy(
            src_ref=src, dst_ref=dst, send_sem=send_sem.at[phase],
            recv_sem=recv_sem.at[phase] if arrival is None else arrival,
            device_id=device, device_id_type=MESH,
        )

    def arrived(ref, phase, arrival=None):
        remote(ref, ref, phase, other_y(1), arrival).wait_recv()

    def scatter(src, dst, phase, arrival=None, pairs=False):
        def send(g, device):
            remote(src.at[g], dst, phase, device, arrival).start()

        each_member(send, pairs)

    most = pl.ds(0, 63)
    sent = [
        gs.at[most], rs.at[most], gb.at[pl.ds(0, 3)], ls.at[most], dls.at[most], drs.at[most],
        wb.at[pl.ds(0, 31)], zb.at[pl.ds(0, 7)], wb.at[pl.ds(0, 31)],
    ]

    def drain(phases):
        for k in phases:
            remote(sent[k], sent[k], k, other_y(1)).wait_send()

    barrier = pltpu.get_barrier_semaphore()

    chips = [lax.rem(lax.div(spot, 2) + d, 4) for d in range(4)]
    ys = [lax.rem(y + d, 4) for d in range(4)]
    hops = {0: 0, 1: 1, 2: 2, 3: 1}
    around = sorted(
        ((d, e) for d in range(4) for e in range(8)), key=lambda t: -hops[t[0]] - hops[t[1] // 2]
    )

    def greet(device):
        pl.semaphore_signal(barrier, inc=1, device_id=device, device_id_type=MESH)

    each_member(lambda g, device: greet(device))

    for d, e in around:
        if d:
            greet((row - spot + spots[e], zhi * 4 + ys[d]))

    loads = [
        pltpu.make_async_copy(cot_hbm, cot_v, load_sem.at[0]),
        pltpu.make_async_copy(pair_hbm, pair_v, load_sem.at[1]),
    ]
    for k, w in enumerate((wl, wlg, wr, wrg)):
        loads.append(pltpu.make_async_copy(w, wst.at[pl.ds(64 * k, 64)], load_sem.at[2 + k]))
    for load in loads:
        load.start()

    loads[0].wait()

    def pack(t, c):
        g = cot_v[pl.ds(t * 8, 8)].astype(F32)
        gs[pl.ds(t * 8, 8)] = jnp.concatenate([g[:, :8], g[:, 8:]], axis=-1).astype(BF)
        return c

    lax.fori_loop(0, 8, pack, 0, unroll=2)
    gb[y, me] = gs[me]
    for load in loads[1:]:
        load.wait()

    def gated(side, b, n):
        pt = lax.dot_general(
            wst[128 * side : 128 * side + 128], n, (((1,), (1,)), ((), ())),
            preferred_element_type=F32,
        )
        q, s = pt[:64], jax.nn.sigmoid(pt[64:])
        v = s * q
        s_s[side, b] = s
        f_s[side, b] = v * (1.0 - s)
        scr[side, pl.ds(b, 64, stride=8), :] = v

    def normalize(b, c):
        x = jnp.concatenate([pair_v[b], pair_v[b + 8]], axis=0).astype(F32)
        cen = x - jnp.mean(x, axis=1, keepdims=True)
        var = jnp.mean(cen * cen, axis=1, keepdims=True)
        inv = jnp.broadcast_to(1.0 / jnp.sqrt(var + 1e-05), (128, 128))
        xh = cen * inv
        n = xh.astype(BF)
        xhat[pl.ds(128 * b, 128)] = xh
        invs[pl.ds(128 * b, 128)] = inv
        nrm[pl.ds(128 * b, 128)] = n
        gated(1, b, n)
        return c

    lax.fori_loop(0, 8, normalize, 0, unroll=4)
    rs[...] = scr[1].reshape(64, 8, 128).astype(BF)
    rb[me] = rs[me]

    def left_too(b, c):
        gated(0, b, nrm[pl.ds(128 * b, 128)])
        return c

    lax.fori_loop(0, 8, left_too, 0, unroll=4)
    ls[...] = scr[0].reshape(64, 8, 128).astype(BF)
    lb[me] = ls[me]
    pl.semaphore_wait(barrier, 87)
    scatter(gs, gb.at[y, me], G_OWN, g_sem.at[z], pairs=True)
    scatter(rs, rb.at[me], R_OWN)
    scatter(ls, lb.at[me], L_OWN)

    def spread(zz):
        block = gb.at[y, pl.ds(zz * 8, 8)]
        for d in (2, 1, 3):
            remote(block, block, G_ALL, other_y(d), gy_sem.at[zz]).start()

    arrived(gb.at[0, pl.ds(0, 7)], G_OWN, g_sem.at[z])
    spread(z)

    def spread_next(k, c):
        zz = paired(k)
        arrived(gb.at[0, pl.ds(0, 8)], G_OWN, g_sem.at[zz])
        spread(zz)
        return c

    lax.fori_loop(1, 8, spread_next, 0)
    low3 = lax.broadcasted_iota(jnp.int32, (8, 8, 128), 2) < 64

    def interleave(a, b):
        a, b = a.astype(F32), b.astype(F32)
        top, bottom = jnp.where(low3, a, swap(b)), jnp.where(low3, swap(a), b)
        return jnp.stack([top, bottom], axis=1).reshape(128, 128).astype(BF)

    def join(side, got):
        for t in range(4):
            mat[side, 128 * t : 128 * t + 128] = interleave(
                got[8 * t : 8 * t + 8], got[32 + 8 * t : 40 + 8 * t]
            )

    def contract(side, first, dst, zl):
        rows = pl.ds(pl.multiple_of(first + zl * 128, 128), 128)
        d = jnp.dot(gg[rows], mat[side], preferred_element_type=F32).reshape(8, 2, 8, 128)
        a, b = d[:, 0], d[:, 1]
        dst[pl.ds(8 * zl, 8)] = jnp.where(low3, a, swap(b)).astype(BF)
        dst[pl.ds(8 * zl + 32, 8)] = jnp.where(low3, swap(a), b).astype(BF)

    def collect(k):
        zz = paired(k)
        arrived(gb.at[0, pl.ds(0, 24)], G_ALL, gy_sem.at[zz])
        src = pl.ds(zz * 8, 8)
        zl, half = lax.rem(zz, 4) * 128, lax.div(zz, 4) * 256
        for q in range(2):
            block = interleave(gb[2 * q, src], gb[2 * q + 1, src])
            i = pl.multiple_of(zl, 128)
            j = pl.multiple_of(half + q * 128, 128)
            gg[pl.ds(i, 128), pl.ds(j, 128)] = block
            gg[pl.ds(512 + j, 128), pl.ds(i, 128)] = block.T

    def give_back(src, dst, phase, p):
        def send(g, device):
            remote(src.at[g], dst, phase, device).start()

        of_z(send, paired(2 * p), range(1 if p == 0 else 0, 8))
        of_z(send, paired(2 * p + 1), range(8))

    for p in range(4):
        if p == 1:
            arrived(lb.at[most], L_OWN)
            join(0, lb)
        collect(2 * p)
        collect(2 * p + 1)
        if p == 0:
            arrived(rb.at[most], R_OWN)
            join(1, rb)
        contract(1, 0, dls, lax.rem(near(p), 4))
        give_back(dls, dlb.at[me], D_LEFT, p)
    dlb[me] = dls[me]
    for p in range(4):
        contract(0, 512, drs, lax.rem(near(p), 4))
        give_back(drs, drb.at[me], D_RIGHT, p)
    drb[me] = drs[me]

    def weigh(side, got):
        scr[side] = got[...].astype(F32).reshape(512, 128)
        e, f = 128 * side, 128 * side + 64
        for b in range(8):
            d = scr[side, pl.ds(b, 64, stride=8), :]
            efs[e : e + 64, 128 * b : 128 * b + 128] = (d * s_s[side, b]).astype(BF)
            efs[f : f + 64, 128 * b : 128 * b + 128] = (d * f_s[side, b]).astype(BF)
        wg = jnp.dot(efs[e : e + 128], nrm[...], preferred_element_type=F32)
        ws[:, side] = wg.reshape(16, 8, 128)

        for d, e in around:
            if e % 2 == 0 and d + e:
                p = ys[d] * 4 + chips[e // 2]
                to = (row - spot + 2 * chips[e // 2] + side, zhi * 4 + ys[d])
                remote(ws.at[p, side], wb.at[place], W_PLANE, to).start()

        @pl.when(core != side)
        def _():
            own = in_plane(2 * pair_of + side)
            remote(ws.at[pair_of, side], wb.at[place], W_PLANE, own).start()

        @pl.when(core == side)
        def _():
            wb[place] = ws[pair_of, side]

    arrived(dlb.at[most], D_LEFT)
    weigh(0, dlb)
    arrived(drb.at[most], D_RIGHT)
    weigh(1, drb)
    for b in range(8):
        dn = lax.dot_general(
            efs[:, 128 * b : 128 * b + 128], wst[...], (((0,), (0,)), ((), ())),
            preferred_element_type=F32,
        )
        xh = xhat[128 * b : 128 * b + 128, :]
        m1 = jnp.mean(dn, axis=1, keepdims=True)
        m2 = jnp.mean(dn * xh, axis=1, keepdims=True)
        pg = ((dn - m1 - xh * m2) * invs[128 * b : 128 * b + 128, :]).astype(BF)
        pg_out[b], pg_out[b + 8] = pg[:64], pg[64:]

    arrived(wb.at[pl.ds(0, 31)], W_PLANE)
    zb[z] = jnp.sum(wb[...], axis=0)
    for d in (4, 3, 5, 2, 6, 1, 7):
        remote(zb.at[z], zb.at[z], W_Z, member(lax.rem(me + 8 * d, 64))).start()
    arrived(zb.at[pl.ds(0, 7)], W_Z)
    ag[pair_of, core] = jnp.sum(zb[...], axis=0) * (1.0 / 512)

    mine = ag.at[pair_of, core]
    for d, e in around:
        if d + e:
            to = (row - spot + spots[e], zhi * 4 + ys[d])
            remote(mine, mine, W_ALL, to).start()
    arrived(wb.at[pl.ds(0, 31)], W_ALL)
    sums_out[0:16] = ag[:, 0]
    sums_out[16:32] = ag[:, 1]
    drain(range(9))


def deliver(pg, sums, out, *rest):
    sem = rest[-1]
    copies = [pltpu.make_async_copy(pg, out, sem.at[0])]
    for k in range(4):
        copies.append(pltpu.make_async_copy(sums.at[pl.ds(8 * k, 8)], rest[k], sem.at[k + 1]))
    for copy in copies:
        copy.start()
    for copy in copies:
        copy.wait()


def shards(pair, cotangent, w_left, w_left_gate, w_right, w_right_gate):
    vm, dma = pltpu.VMEM, pltpu.SemaphoreType.DMA
    chunk = vm((64, 8, 128), BF)
    pg, sums = pl.pallas_call(
        kernel,
        out_shape=[vm((16, 64, 128), BF), vm((32, 8, 128), F32)],
        in_specs=[pl.BlockSpec(memory_space=pl.ANY)] * 6,
        out_specs=[pl.BlockSpec(memory_space=vm)] * 2,
        scratch_shapes=[
            vm((16, 64, 128), BF),
            vm((64, 16, 64), BF),
            vm((256, 128), BF),
            vm((1024, 128), F32),
            vm((1024, 128), F32),
            vm((1024, 128), BF),
            vm((2, 512, 128), F32),
            vm((2, 8, 64, 128), F32),
            vm((2, 8, 64, 128), F32),
            chunk,
            vm((4, 64, 8, 128), BF),
            vm((1024, 512), BF),
            chunk, chunk, chunk, chunk,
            vm((2, 512, 128), BF),
            chunk, chunk, chunk, chunk,
            vm((256, 1024), BF),
            vm((16, 2, 8, 128), F32),
            vm((32, 8, 128), F32),
            vm((8, 8, 128), F32),
            vm((16, 2, 8, 128), F32),
            dma((6,)), dma((9,)), dma((9,)), dma((8,)), dma((8,)),
        ],
        compiler_params=pltpu.CompilerParams(collective_id=0, has_side_effects=True),
    )(pair, cotangent, w_left.T, w_left_gate.T, w_right.T, w_right_gate.T)
    keep = pltpu.with_memory_space_constraint
    grad = jax.ShapeDtypeStruct((8, 8, 128), F32)
    out, *grads = pl.pallas_call(
        deliver,
        out_shape=[jax.ShapeDtypeStruct((16, 64, 128), BF), grad, grad, grad, grad],
        in_specs=[pl.BlockSpec(memory_space=vm)] * 2,
        out_specs=[pl.BlockSpec(memory_space=pl.ANY)] * 5,
        scratch_shapes=[dma((5,))],
    )(keep(pg, vm), keep(sums, vm))
    return (out, *(g.reshape(64, 128).T for g in grads))


def solution(mesh):
    in_specs = (P("row", "col", None), P(None, "row", "col"), P(), P(), P(), P())
    out_specs = (P("row", "col", None), P(), P(), P(), P())
    return jax.shard_map(shards, mesh=mesh, in_specs=in_specs, out_specs=out_specs, check_vma=False)
```

```python
import jax
import jax.numpy as jnp
from jax import lax
from jax.experimental import pallas as pl
from jax.experimental.pallas import tpu as pltpu
from jax.sharding import PartitionSpec as P

MESH = pl.DeviceIdType.MESH
BF, F32 = jnp.bfloat16, jnp.float32

G_OWN, R_OWN, G_ALL, L_OWN, D_LEFT, D_RIGHT, W_PLANE, W_Z, W_ALL = range(9)


def swap(v):
    return pltpu.roll(v, 64, v.ndim - 1)


def kernel(
    pair_hbm, cot_hbm, wl, wlg, wr, wrg, pg_out, sums_out,
    pair_v, cot_v, wst, xhat, invs, nrm, scr, s_s, f_s,
    gs, gb, gg, rs, rb, ls, lb, mat, dls, dlb, drs, drb, efs, ws, wb, zb, ag,
    load_sem, send_sem, recv_sem, g_sem, gy_sem,
):
    row, col = lax.axis_index("row"), lax.axis_index("col")
    zhi, y = lax.div(col, 4), lax.rem(col, 4)
    z, spot = zhi * 4 + lax.div(row, 8), lax.rem(row, 8)
    core = lax.rem(spot, 2)
    me = z * 8 + spot
    place = y * 8 + spot
    pair_of = lax.div(place, 2)

    def member(g):
        return (lax.rem(g, 32), lax.div(g, 32) * 4 + y)

    def other_y(d):
        return (row, zhi * 4 + lax.rem(y + d, 4))

    def in_plane(p):
        return (row - spot + lax.rem(p, 8), zhi * 4 + lax.div(p, 8))

    spots = [lax.rem(spot + e, 8) for e in range(8)]

    def near(k):
        return lax.rem(z + 8 + (2 * lax.rem(k, 2) - 1) * lax.div(k + 1, 2), 8)

    def paired(k):
        return lax.rem(near(lax.div(k, 2)) + 4 * lax.rem(k, 2), 8)

    def far(k):
        return lax.rem(z + 4 + (1 - 2 * lax.rem(k, 2)) * lax.div(k + 1, 2), 8)

    def of_z(act, zz, turn):
        r, c = lax.rem(zz, 4) * 8, lax.div(zz, 4) * 4 + y
        for e in turn:
            act(zz * 8 + spots[e], (r + spots[e], c))

    def each_member(act, pairs=False):
        def step(k, carry):
            of_z(act, paired(k + 1) if pairs else far(k), range(8))
            return carry

        if pairs:
            of_z(act, z, range(1, 8))
        lax.fori_loop(0, 7, step, 0)
        if not pairs:
            of_z(act, z, range(1, 8))

    def remote(src, dst, phase, device, arrival=None):
        return pltpu.make_async_remote_copy(
            src_ref=src, dst_ref=dst, send_sem=send_sem.at[phase],
            recv_sem=recv_sem.at[phase] if arrival is None else arrival,
            device_id=device, device_id_type=MESH,
        )

    def arrived(ref, phase, arrival=None):
        remote(ref, ref, phase, other_y(1), arrival).wait_recv()

    def scatter(src, dst, phase, arrival=None, pairs=False):
        def send(g, device):
            remote(src.at[g], dst, phase, device, arrival).start()

        each_member(send, pairs)

    most = pl.ds(0, 63)
    sent = [
        gs.at[most], rs.at[most], gb.at[pl.ds(0, 3)], ls.at[most], dls.at[most], drs.at[most],
        wb.at[pl.ds(0, 31)], zb.at[pl.ds(0, 7)], wb.at[pl.ds(0, 31)],
    ]

    def drain(phases):
        for k in phases:
            remote(sent[k], sent[k], k, other_y(1)).wait_send()

    loads = [
        pltpu.make_async_copy(cot_hbm, cot_v, load_sem.at[0]),
        pltpu.make_async_copy(pair_hbm, pair_v, load_sem.at[1]),
    ]
    for k, w in enumerate((wl, wlg, wr, wrg)):
        loads.append(pltpu.make_async_copy(w, wst.at[pl.ds(64 * k, 64)], load_sem.at[2 + k]))
    for load in loads:
        load.start()

    barrier = pltpu.get_barrier_semaphore()

    chips = [lax.rem(lax.div(spot, 2) + d, 4) for d in range(4)]
    ys = [lax.rem(y + d, 4) for d in range(4)]
    hops = {0: 0, 1: 1, 2: 2, 3: 1}
    around = sorted(
        ((d, e) for d in range(4) for e in range(8)), key=lambda t: -hops[t[0]] - hops[t[1] // 2]
    )

    def greet(device):
        pl.semaphore_signal(barrier, inc=1, device_id=device, device_id_type=MESH)

    each_member(lambda g, device: greet(device))

    for d, e in around:
        if d:
            greet((row - spot + spots[e], zhi * 4 + ys[d]))

    loads[0].wait()

    def pack(t, c):
        g = cot_v[pl.ds(t * 8, 8)].astype(F32)
        gs[pl.ds(t * 8, 8)] = jnp.concatenate([g[:, :8], g[:, 8:]], axis=-1).astype(BF)
        return c

    lax.fori_loop(0, 8, pack, 0, unroll=2)
    gb[y, me] = gs[me]
    for load in loads[1:]:
        load.wait()

    def gated(side, b, n):
        pt = lax.dot_general(
            wst[128 * side : 128 * side + 128], n, (((1,), (1,)), ((), ())),
            preferred_element_type=F32,
        )
        q, s = pt[:64], jax.nn.sigmoid(pt[64:])
        v = s * q
        s_s[side, b] = s
        f_s[side, b] = v * (1.0 - s)
        scr[side, pl.ds(b, 64, stride=8), :] = v

    def normalize(b, c):
        x = jnp.concatenate([pair_v[b], pair_v[b + 8]], axis=0).astype(F32)
        cen = x - jnp.mean(x, axis=1, keepdims=True)
        var = jnp.mean(cen * cen, axis=1, keepdims=True)
        inv = jnp.broadcast_to(1.0 / jnp.sqrt(var + 1e-05), (128, 128))
        xh = cen * inv
        n = xh.astype(BF)
        xhat[pl.ds(128 * b, 128)] = xh
        invs[pl.ds(128 * b, 128)] = inv
        nrm[pl.ds(128 * b, 128)] = n
        gated(1, b, n)
        return c

    lax.fori_loop(0, 8, normalize, 0, unroll=4)
    rs[...] = scr[1].reshape(64, 8, 128).astype(BF)
    rb[me] = rs[me]

    def left_too(b, c):
        gated(0, b, nrm[pl.ds(128 * b, 128)])
        return c

    lax.fori_loop(0, 8, left_too, 0, unroll=4)
    ls[...] = scr[0].reshape(64, 8, 128).astype(BF)
    lb[me] = ls[me]
    pl.semaphore_wait(barrier, 87)
    scatter(gs, gb.at[y, me], G_OWN, g_sem.at[z], pairs=True)
    scatter(rs, rb.at[me], R_OWN, pairs=True)
    scatter(ls, lb.at[me], L_OWN, pairs=True)

    def spread(zz):
        block = gb.at[y, pl.ds(zz * 8, 8)]
        for d in (2, 1, 3):
            remote(block, block, G_ALL, other_y(d), gy_sem.at[zz]).start()

    arrived(gb.at[0, pl.ds(0, 7)], G_OWN, g_sem.at[z])
    spread(z)

    def spread_next(k, c):
        zz = paired(k)
        arrived(gb.at[0, pl.ds(0, 8)], G_OWN, g_sem.at[zz])
        spread(zz)
        return c

    lax.fori_loop(1, 8, spread_next, 0)
    low3 = lax.broadcasted_iota(jnp.int32, (8, 8, 128), 2) < 64

    def interleave(a, b):
        a, b = a.astype(F32), b.astype(F32)
        top, bottom = jnp.where(low3, a, swap(b)), jnp.where(low3, swap(a), b)
        return jnp.stack([top, bottom], axis=1).reshape(128, 128).astype(BF)

    def join(side, got):
        for t in range(4):
            mat[side, 128 * t : 128 * t + 128] = interleave(
                got[8 * t : 8 * t + 8], got[32 + 8 * t : 40 + 8 * t]
            )

    def contract(side, first, dst, zl):
        rows = pl.ds(pl.multiple_of(first + zl * 128, 128), 128)
        d = jnp.dot(gg[rows], mat[side], preferred_element_type=F32).reshape(8, 2, 8, 128)
        a, b = d[:, 0], d[:, 1]
        dst[pl.ds(8 * zl, 8)] = jnp.where(low3, a, swap(b)).astype(BF)
        dst[pl.ds(8 * zl + 32, 8)] = jnp.where(low3, swap(a), b).astype(BF)

    def collect(k):
        zz = paired(k)
        arrived(gb.at[0, pl.ds(0, 24)], G_ALL, gy_sem.at[zz])
        src = pl.ds(zz * 8, 8)
        zl, half = lax.rem(zz, 4) * 128, lax.div(zz, 4) * 256
        for q in range(2):
            block = interleave(gb[2 * q, src], gb[2 * q + 1, src])
            i = pl.multiple_of(zl, 128)
            j = pl.multiple_of(half + q * 128, 128)
            gg[pl.ds(i, 128), pl.ds(j, 128)] = block
            gg[pl.ds(512 + j, 128), pl.ds(i, 128)] = block.T

    def give_back(src, dst, phase, p):
        def send(g, device):
            remote(src.at[g], dst, phase, device).start()

        of_z(send, paired(2 * p), range(1 if p == 0 else 0, 8))
        of_z(send, paired(2 * p + 1), range(8))

    for p in range(4):
        if p == 1:
            arrived(lb.at[most], L_OWN)
            join(0, lb)
        collect(2 * p)
        collect(2 * p + 1)
        if p == 0:
            arrived(rb.at[most], R_OWN)
            join(1, rb)
        contract(1, 0, dls, lax.rem(near(p), 4))
        give_back(dls, dlb.at[me], D_LEFT, p)
    dlb[me] = dls[me]
    d = jnp.dot(gg[512:], mat[0], preferred_element_type=F32).reshape(32, 2, 8, 128)
    low4 = lax.broadcasted_iota(jnp.int32, (32, 8, 128), 2) < 64
    drs[0:32] = jnp.where(low4, d[:, 0], swap(d[:, 1])).astype(BF)
    drs[32:64] = jnp.where(low4, swap(d[:, 0]), d[:, 1]).astype(BF)
    scatter(drs, drb.at[me], D_RIGHT)
    drb[me] = drs[me]

    def weigh(side, got):
        scr[side] = got[...].astype(F32).reshape(512, 128)
        e, f = 128 * side, 128 * side + 64
        for b in range(8):
            d = scr[side, pl.ds(b, 64, stride=8), :]
            efs[e : e + 64, 128 * b : 128 * b + 128] = (d * s_s[side, b]).astype(BF)
            efs[f : f + 64, 128 * b : 128 * b + 128] = (d * f_s[side, b]).astype(BF)
        wg = jnp.dot(efs[e : e + 128], nrm[...], preferred_element_type=F32)
        ws[:, side] = wg.reshape(16, 8, 128)

        for d, e in around:
            if e % 2 == 0 and d + e:
                p = ys[d] * 4 + chips[e // 2]
                to = (row - spot + 2 * chips[e // 2] + side, zhi * 4 + ys[d])
                remote(ws.at[p, side], wb.at[place], W_PLANE, to).start()

        @pl.when(core != side)
        def _():
            own = in_plane(2 * pair_of + side)
            remote(ws.at[pair_of, side], wb.at[place], W_PLANE, own).start()

        @pl.when(core == side)
        def _():
            wb[place] = ws[pair_of, side]

    arrived(dlb.at[most], D_LEFT)
    weigh(0, dlb)
    arrived(drb.at[most], D_RIGHT)
    weigh(1, drb)
    for b in range(8):
        dn = lax.dot_general(
            efs[:, 128 * b : 128 * b + 128], wst[...], (((0,), (0,)), ((), ())),
            preferred_element_type=F32,
        )
        xh = xhat[128 * b : 128 * b + 128, :]
        m1 = jnp.mean(dn, axis=1, keepdims=True)
        m2 = jnp.mean(dn * xh, axis=1, keepdims=True)
        pg = ((dn - m1 - xh * m2) * invs[128 * b : 128 * b + 128, :]).astype(BF)
        pg_out[b], pg_out[b + 8] = pg[:64], pg[64:]

    arrived(wb.at[pl.ds(0, 31)], W_PLANE)
    zb[z] = jnp.sum(wb[...], axis=0)
    for d in (4, 3, 5, 2, 6, 1, 7):
        remote(zb.at[z], zb.at[z], W_Z, member(lax.rem(me + 8 * d, 64))).start()
    arrived(zb.at[pl.ds(0, 7)], W_Z)
    ag[pair_of, core] = jnp.sum(zb[...], axis=0) * (1.0 / 512)

    mine = ag.at[pair_of, core]
    for d, e in around:
        if d + e:
            to = (row - spot + spots[e], zhi * 4 + ys[d])
            remote(mine, mine, W_ALL, to).start()
    arrived(wb.at[pl.ds(0, 31)], W_ALL)
    sums_out[0:16] = ag[:, 0]
    sums_out[16:32] = ag[:, 1]
    drain(range(9))


def deliver(pg, sums, out, *rest):
    sem = rest[-1]
    copies = [pltpu.make_async_copy(pg, out, sem.at[0])]
    for k in range(4):
        copies.append(pltpu.make_async_copy(sums.at[pl.ds(8 * k, 8)], rest[k], sem.at[k + 1]))
    for copy in copies:
        copy.start()
    for copy in copies:
        copy.wait()


def shards(pair, cotangent, w_left, w_left_gate, w_right, w_right_gate):
    vm, dma = pltpu.VMEM, pltpu.SemaphoreType.DMA
    chunk = vm((64, 8, 128), BF)
    pg, sums = pl.pallas_call(
        kernel,
        out_shape=[vm((16, 64, 128), BF), vm((32, 8, 128), F32)],
        in_specs=[pl.BlockSpec(memory_space=pl.ANY)] * 6,
        out_specs=[pl.BlockSpec(memory_space=vm)] * 2,
        scratch_shapes=[
            vm((16, 64, 128), BF),
            vm((64, 16, 64), BF),
            vm((256, 128), BF),
            vm((1024, 128), F32),
            vm((1024, 128), F32),
            vm((1024, 128), BF),
            vm((2, 512, 128), F32),
            vm((2, 8, 64, 128), F32),
            vm((2, 8, 64, 128), F32),
            chunk,
            vm((4, 64, 8, 128), BF),
            vm((1024, 512), BF),
            chunk, chunk, chunk, chunk,
            vm((2, 512, 128), BF),
            chunk, chunk, chunk, chunk,
            vm((256, 1024), BF),
            vm((16, 2, 8, 128), F32),
            vm((32, 8, 128), F32),
            vm((8, 8, 128), F32),
            vm((16, 2, 8, 128), F32),
            dma((6,)), dma((9,)), dma((9,)), dma((8,)), dma((8,)),
        ],
        compiler_params=pltpu.CompilerParams(collective_id=0, has_side_effects=True),
    )(pair, cotangent, w_left.T, w_left_gate.T, w_right.T, w_right_gate.T)
    keep = pltpu.with_memory_space_constraint
    grad = jax.ShapeDtypeStruct((8, 8, 128), F32)
    out, *grads = pl.pallas_call(
        deliver,
        out_shape=[jax.ShapeDtypeStruct((16, 64, 128), BF), grad, grad, grad, grad],
        in_specs=[pl.BlockSpec(memory_space=vm)] * 2,
        out_specs=[pl.BlockSpec(memory_space=pl.ANY)] * 5,
        scratch_shapes=[dma((5,))],
    )(keep(pg, vm), keep(sums, vm))
    return (out, *(g.reshape(64, 128).T for g in grads))


def solution(mesh):
    in_specs = (P("row", "col", None), P(None, "row", "col"), P(), P(), P(), P())
    out_specs = (P("row", "col", None), P(), P(), P(), P())
    return jax.shard_map(shards, mesh=mesh, in_specs=in_specs, out_specs=out_specs, check_vma=False)
```

```python
import jax
import jax.numpy as jnp
from jax import lax
from jax.experimental import pallas as pl
from jax.experimental.pallas import tpu as pltpu
from jax.sharding import PartitionSpec as P

MESH = pl.DeviceIdType.MESH
BF, F32 = jnp.bfloat16, jnp.float32

G_OWN, R_OWN, G_ALL, L_OWN, D_LEFT, D_RIGHT, W_PLANE, W_Z, W_ALL = range(9)


def swap(v):
    return pltpu.roll(v, 64, v.ndim - 1)


def kernel(
    pair_hbm, cot_hbm, wl, wlg, wr, wrg, pg_out, sums_out,
    pair_v, cot_v, wst, xhat, invs, nrm, scr, s_s, f_s,
    gs, gb, gg, rs, rb, ls, lb, mat, dls, dlb, drs, drb, efs, ws, wb, zb, ag,
    load_sem, send_sem, recv_sem, g_sem, gy_sem,
):
    row, col = lax.axis_index("row"), lax.axis_index("col")
    zhi, y = lax.div(col, 4), lax.rem(col, 4)
    z, spot = zhi * 4 + lax.div(row, 8), lax.rem(row, 8)
    core = lax.rem(spot, 2)
    me = z * 8 + spot
    place = y * 8 + spot
    pair_of = lax.div(place, 2)

    def member(g):
        return (lax.rem(g, 32), lax.div(g, 32) * 4 + y)

    def other_y(d):
        return (row, zhi * 4 + lax.rem(y + d, 4))

    def in_plane(p):
        return (row - spot + lax.rem(p, 8), zhi * 4 + lax.div(p, 8))

    spots = [lax.rem(spot + e, 8) for e in range(8)]

    def near(k):
        return lax.rem(z + 8 + (2 * lax.rem(k, 2) - 1) * lax.div(k + 1, 2), 8)

    def paired(k):
        return lax.rem(near(lax.div(k, 2)) + 4 * lax.rem(k, 2), 8)

    def far(k):
        return lax.rem(z + 4 + (1 - 2 * lax.rem(k, 2)) * lax.div(k + 1, 2), 8)

    def of_z(act, zz, turn):
        r, c = lax.rem(zz, 4) * 8, lax.div(zz, 4) * 4 + y
        for e in turn:
            act(zz * 8 + spots[e], (r + spots[e], c))

    def each_member(act, pairs=False):
        def step(k, carry):
            of_z(act, paired(k + 1) if pairs else far(k), range(8))
            return carry

        if pairs:
            of_z(act, z, range(1, 8))
        lax.fori_loop(0, 7, step, 0)
        if not pairs:
            of_z(act, z, range(1, 8))

    def remote(src, dst, phase, device, arrival=None):
        return pltpu.make_async_remote_copy(
            src_ref=src, dst_ref=dst, send_sem=send_sem.at[phase],
            recv_sem=recv_sem.at[phase] if arrival is None else arrival,
            device_id=device, device_id_type=MESH,
        )

    def arrived(ref, phase, arrival=None):
        remote(ref, ref, phase, other_y(1), arrival).wait_recv()

    def scatter(src, dst, phase, arrival=None, pairs=False):
        def send(g, device):
            remote(src.at[g], dst, phase, device, arrival).start()

        each_member(send, pairs)

    most = pl.ds(0, 63)
    sent = [
        gs.at[most], rs.at[most], gb.at[pl.ds(0, 3)], ls.at[most], dls.at[most], drs.at[most],
        wb.at[pl.ds(0, 31)], zb.at[pl.ds(0, 7)], wb.at[pl.ds(0, 31)],
    ]

    def drain(phases):
        for k in phases:
            remote(sent[k], sent[k], k, other_y(1)).wait_send()

    loads = [
        pltpu.make_async_copy(cot_hbm, cot_v, load_sem.at[0]),
        pltpu.make_async_copy(pair_hbm, pair_v, load_sem.at[1]),
    ]
    for k, w in enumerate((wl, wlg, wr, wrg)):
        loads.append(pltpu.make_async_copy(w, wst.at[pl.ds(64 * k, 64)], load_sem.at[2 + k]))
    for load in loads:
        load.start()

    barrier = pltpu.get_barrier_semaphore()

    chips = [lax.rem(lax.div(spot, 2) + d, 4) for d in range(4)]
    ys = [lax.rem(y + d, 4) for d in range(4)]
    hops = {0: 0, 1: 1, 2: 2, 3: 1}
    around = sorted(
        ((d, e) for d in range(4) for e in range(8)), key=lambda t: -hops[t[0]] - hops[t[1] // 2]
    )

    def greet(device):
        pl.semaphore_signal(barrier, inc=1, device_id=device, device_id_type=MESH)

    each_member(lambda g, device: greet(device))

    for d, e in around:
        if d:
            greet((row - spot + spots[e], zhi * 4 + ys[d]))

    loads[0].wait()

    def pack(t, c):
        g = cot_v[pl.ds(t * 8, 8)].astype(F32)
        gs[pl.ds(t * 8, 8)] = jnp.concatenate([g[:, :8], g[:, 8:]], axis=-1).astype(BF)
        return c

    lax.fori_loop(0, 8, pack, 0, unroll=2)
    gb[y, me] = gs[me]
    for load in loads[1:]:
        load.wait()

    def gated(side, b, n):
        pt = lax.dot_general(
            wst[128 * side : 128 * side + 128], n, (((1,), (1,)), ((), ())),
            preferred_element_type=F32,
        )
        q, s = pt[:64], jax.nn.sigmoid(pt[64:])
        v = s * q
        s_s[side, b] = s
        f_s[side, b] = v * (1.0 - s)
        scr[side, pl.ds(b, 64, stride=8), :] = v

    def normalize(b, c):
        x = jnp.concatenate([pair_v[b], pair_v[b + 8]], axis=0).astype(F32)
        cen = x - jnp.mean(x, axis=1, keepdims=True)
        var = jnp.mean(cen * cen, axis=1, keepdims=True)
        inv = jnp.broadcast_to(1.0 / jnp.sqrt(var + 1e-05), (128, 128))
        xh = cen * inv
        n = xh.astype(BF)
        xhat[pl.ds(128 * b, 128)] = xh
        invs[pl.ds(128 * b, 128)] = inv
        nrm[pl.ds(128 * b, 128)] = n
        gated(1, b, n)
        return c

    lax.fori_loop(0, 8, normalize, 0, unroll=4)
    rs[...] = scr[1].reshape(64, 8, 128).astype(BF)
    rb[me] = rs[me]

    def left_too(b, c):
        gated(0, b, nrm[pl.ds(128 * b, 128)])
        return c

    lax.fori_loop(0, 8, left_too, 0, unroll=4)
    ls[...] = scr[0].reshape(64, 8, 128).astype(BF)
    lb[me] = ls[me]
    pl.semaphore_wait(barrier, 87)
    scatter(gs, gb.at[y, me], G_OWN, g_sem.at[z], pairs=True)
    scatter(rs, rb.at[me], R_OWN, pairs=True)
    scatter(ls, lb.at[me], L_OWN, pairs=True)

    def spread(zz):
        block = gb.at[y, pl.ds(zz * 8, 8)]
        for d in (2, 1, 3):
            remote(block, block, G_ALL, other_y(d), gy_sem.at[zz]).start()

    arrived(gb.at[0, pl.ds(0, 7)], G_OWN, g_sem.at[z])
    spread(z)

    def spread_next(k, c):
        zz = paired(k)
        arrived(gb.at[0, pl.ds(0, 8)], G_OWN, g_sem.at[zz])
        spread(zz)
        return c

    lax.fori_loop(1, 8, spread_next, 0)
    low3 = lax.broadcasted_iota(jnp.int32, (8, 8, 128), 2) < 64

    def interleave(a, b):
        a, b = a.astype(F32), b.astype(F32)
        top, bottom = jnp.where(low3, a, swap(b)), jnp.where(low3, swap(a), b)
        return jnp.stack([top, bottom], axis=1).reshape(128, 128).astype(BF)

    def join(side, got):
        for t in range(4):
            mat[side, 128 * t : 128 * t + 128] = interleave(
                got[8 * t : 8 * t + 8], got[32 + 8 * t : 40 + 8 * t]
            )

    def contract(side, first, dst, zl):
        rows = pl.ds(pl.multiple_of(first + zl * 128, 128), 128)
        d = jnp.dot(gg[rows], mat[side], preferred_element_type=F32).reshape(8, 2, 8, 128)
        a, b = d[:, 0], d[:, 1]
        dst[pl.ds(8 * zl, 8)] = jnp.where(low3, a, swap(b)).astype(BF)
        dst[pl.ds(8 * zl + 32, 8)] = jnp.where(low3, swap(a), b).astype(BF)

    def collect(k):
        zz = paired(k)
        arrived(gb.at[0, pl.ds(0, 24)], G_ALL, gy_sem.at[zz])
        src = pl.ds(zz * 8, 8)
        zl, half = lax.rem(zz, 4) * 128, lax.div(zz, 4) * 256
        for q in range(2):
            block = interleave(gb[2 * q, src], gb[2 * q + 1, src])
            i = pl.multiple_of(zl, 128)
            j = pl.multiple_of(half + q * 128, 128)
            gg[pl.ds(i, 128), pl.ds(j, 128)] = block
            gg[pl.ds(512 + j, 128), pl.ds(i, 128)] = block.T

    def give_back(src, dst, phase, p):
        def send(g, device):
            remote(src.at[g], dst, phase, device).start()

        of_z(send, paired(2 * p), range(1 if p == 0 else 0, 8))
        of_z(send, paired(2 * p + 1), range(8))

    for p in range(4):
        if p == 1:
            arrived(lb.at[most], L_OWN)
            join(0, lb)
        collect(2 * p)
        collect(2 * p + 1)
        if p == 0:
            arrived(rb.at[most], R_OWN)
            join(1, rb)
        contract(1, 0, dls, lax.rem(near(p), 4))
        give_back(dls, dlb.at[me], D_LEFT, p)
    dlb[me] = dls[me]
    d = jnp.dot(gg[512:], mat[0], preferred_element_type=F32).reshape(32, 2, 8, 128)
    low4 = lax.broadcasted_iota(jnp.int32, (32, 8, 128), 2) < 64
    drs[0:32] = jnp.where(low4, d[:, 0], swap(d[:, 1])).astype(BF)
    drs[32:64] = jnp.where(low4, swap(d[:, 0]), d[:, 1]).astype(BF)
    scatter(drs, drb.at[me], D_RIGHT)
    drb[me] = drs[me]

    def weigh(side, got):
        scr[side] = got[...].astype(F32).reshape(512, 128)
        e, f = 128 * side, 128 * side + 64
        for b in range(8):
            d = scr[side, pl.ds(b, 64, stride=8), :]
            efs[e : e + 64, 128 * b : 128 * b + 128] = (d * s_s[side, b]).astype(BF)
            efs[f : f + 64, 128 * b : 128 * b + 128] = (d * f_s[side, b]).astype(BF)
        wg = jnp.dot(efs[e : e + 128], nrm[...], preferred_element_type=F32)
        ws[:, side] = wg.reshape(16, 8, 128)

        for d, e in around:
            if e % 2 == 0 and d + e:
                p = ys[d] * 4 + chips[e // 2]
                to = (row - spot + 2 * chips[e // 2] + side, zhi * 4 + ys[d])
                remote(ws.at[p, side], wb.at[place], W_PLANE, to).start()

        @pl.when(core != side)
        def _():
            own = in_plane(2 * pair_of + side)
            remote(ws.at[pair_of, side], wb.at[place], W_PLANE, own).start()

        @pl.when(core == side)
        def _():
            wb[place] = ws[pair_of, side]

    arrived(dlb.at[most], D_LEFT)
    weigh(0, dlb)
    arrived(drb.at[most], D_RIGHT)
    weigh(1, drb)
    for b in range(4):
        dn = lax.dot_general(
            efs[:, 128 * b : 128 * b + 128], wst[...], (((0,), (0,)), ((), ())),
            preferred_element_type=F32,
        )
        xh = xhat[128 * b : 128 * b + 128, :]
        m1 = jnp.mean(dn, axis=1, keepdims=True)
        m2 = jnp.mean(dn * xh, axis=1, keepdims=True)
        pg = ((dn - m1 - xh * m2) * invs[128 * b : 128 * b + 128, :]).astype(BF)
        pg_out[b], pg_out[b + 8] = pg[:64], pg[64:]

    arrived(wb.at[pl.ds(0, 31)], W_PLANE)
    zb[z] = jnp.sum(wb[...], axis=0)
    for d in (4, 3, 5, 2, 6, 1, 7):
        remote(zb.at[z], zb.at[z], W_Z, member(lax.rem(me + 8 * d, 64))).start()
    for b in range(4, 8):
        dn = lax.dot_general(
            efs[:, 128 * b : 128 * b + 128], wst[...], (((0,), (0,)), ((), ())),
            preferred_element_type=F32,
        )
        xh = xhat[128 * b : 128 * b + 128, :]
        m1 = jnp.mean(dn, axis=1, keepdims=True)
        m2 = jnp.mean(dn * xh, axis=1, keepdims=True)
        pg = ((dn - m1 - xh * m2) * invs[128 * b : 128 * b + 128, :]).astype(BF)
        pg_out[b], pg_out[b + 8] = pg[:64], pg[64:]

    arrived(zb.at[pl.ds(0, 7)], W_Z)
    ag[pair_of, core] = jnp.sum(zb[...], axis=0) * (1.0 / 512)

    mine = ag.at[pair_of, core]
    for d, e in around:
        if d + e:
            to = (row - spot + spots[e], zhi * 4 + ys[d])
            remote(mine, mine, W_ALL, to).start()
    arrived(wb.at[pl.ds(0, 31)], W_ALL)
    sums_out[0:16] = ag[:, 0]
    sums_out[16:32] = ag[:, 1]
    drain(range(9))


def deliver(pg, sums, out, *rest):
    sem = rest[-1]
    copies = [pltpu.make_async_copy(pg, out, sem.at[0])]
    for k in range(4):
        copies.append(pltpu.make_async_copy(sums.at[pl.ds(8 * k, 8)], rest[k], sem.at[k + 1]))
    for copy in copies:
        copy.start()
    for copy in copies:
        copy.wait()


def shards(pair, cotangent, w_left, w_left_gate, w_right, w_right_gate):
    vm, dma = pltpu.VMEM, pltpu.SemaphoreType.DMA
    chunk = vm((64, 8, 128), BF)
    pg, sums = pl.pallas_call(
        kernel,
        out_shape=[vm((16, 64, 128), BF), vm((32, 8, 128), F32)],
        in_specs=[pl.BlockSpec(memory_space=pl.ANY)] * 6,
        out_specs=[pl.BlockSpec(memory_space=vm)] * 2,
        scratch_shapes=[
            vm((16, 64, 128), BF),
            vm((64, 16, 64), BF),
            vm((256, 128), BF),
            vm((1024, 128), F32),
            vm((1024, 128), F32),
            vm((1024, 128), BF),
            vm((2, 512, 128), F32),
            vm((2, 8, 64, 128), F32),
            vm((2, 8, 64, 128), F32),
            chunk,
            vm((4, 64, 8, 128), BF),
            vm((1024, 512), BF),
            chunk, chunk, chunk, chunk,
            vm((2, 512, 128), BF),
            chunk, chunk, chunk, chunk,
            vm((256, 1024), BF),
            vm((16, 2, 8, 128), F32),
            vm((32, 8, 128), F32),
            vm((8, 8, 128), F32),
            vm((16, 2, 8, 128), F32),
            dma((6,)), dma((9,)), dma((9,)), dma((8,)), dma((8,)),
        ],
        compiler_params=pltpu.CompilerParams(collective_id=0, has_side_effects=True),
    )(pair, cotangent, w_left.T, w_left_gate.T, w_right.T, w_right_gate.T)
    keep = pltpu.with_memory_space_constraint
    grad = jax.ShapeDtypeStruct((8, 8, 128), F32)
    out, *grads = pl.pallas_call(
        deliver,
        out_shape=[jax.ShapeDtypeStruct((16, 64, 128), BF), grad, grad, grad, grad],
        in_specs=[pl.BlockSpec(memory_space=vm)] * 2,
        out_specs=[pl.BlockSpec(memory_space=pl.ANY)] * 5,
        scratch_shapes=[dma((5,))],
    )(keep(pg, vm), keep(sums, vm))
    return (out, *(g.reshape(64, 128).T for g in grads))


def solution(mesh):
    in_specs = (P("row", "col", None), P(None, "row", "col"), P(), P(), P(), P())
    out_specs = (P("row", "col", None), P(), P(), P(), P())
    return jax.shard_map(shards, mesh=mesh, in_specs=in_specs, out_specs=out_specs, check_vma=False)
```
